128 devices in a mesh: wide: 16 (over x, z), narrow: 8 (over y, core).
Axes of the slice: x: 4, y: 4, z: 4, core: 2. Of those that a mesh axis runs over, the one named last changes fastest.
Arguments:
- user_table: bfloat16 [65536, 256], P('wide'), may hold values from -3 to 3
- item_table: bfloat16 [32768, 256], P('wide'), may hold values from -3 to 3
- week_table: bfloat16 [1024, 256], P('wide'), may hold values from -3 to 3
- profile: bfloat16 [65536, 4096], P('wide', 'narrow'), may hold values from -6 to 6
- feature_table: bfloat16 [4096, 256], P('narrow'), may hold values from -0.375 to 0.375
- user_req: int32 [128, 16, 32], P(('wide', 'narrow')), may hold values from 0 to 4095
- item_req: int32 [128, 16, 32], P(('wide', 'narrow')), may hold values from 0 to 2047
- week_req: int32 [128, 16, 4], P(('wide', 'narrow')), may hold values from 0 to 63
- user_counts: int32 [128, 16], P(('wide', 'narrow')), may hold values from 1 to 32, 256 in all within a row
- item_counts: int32 [128, 16], P(('wide', 'narrow')), may hold values from 1 to 32, 256 in all within a row
- week_counts: int32 [128, 16], P(('wide', 'narrow')), may hold values from 1 to 4, 28 in all within a row
- pos_cells: int32 [128, 4096], P(('wide', 'narrow')), may hold values from 0 to 1835007
Outputs:
- grad_users: float32 [65536, 256], P(('wide', 'narrow'))
- grad_items: float32 [32768, 256], P(('wide', 'narrow'))
- grad_weeks: float32 [1024, 256], P(('wide', 'narrow'))
- grad_features: float32 [4096, 256], P('narrow')
The draws below stay inside these ranges and needn't reach their ends.
Inputs may be any that keep to these rules, and one draw needn't show every extreme that they name: `user_req`: only the first user_counts[d, o] slots of owner o are read; the rest hold arbitrary row numbers. Rows may repeat. `item_req`: only the first item_counts[d, o] slots of owner o are read. `week_req`: only the first week_counts[d, o] slots of owner o are read. `user_counts`: each block's counts sum to 256; every block has an owner with exactly 32. `item_counts`: each block's counts sum to 256; every block has an owner with exactly 32. `week_counts`: each block's counts sum to 28; every block has an owner with exactly 4. `pos_cells`: cells may repeat.
All inputs are finite; a program needn't handle non-finite values.
Results may differ from the reference program's by a relative error of at most 0.0015.
Values may be sent and summed in bfloat16 or wider, within the bound.
A program may use at most 128 MiB of HBM per device.

```python
import math
import jax
import jax.numpy as jnp
import numpy as np
from jax import lax

RANK = 256
FEAT = 4096
BU = 256
BI = 256
BW = 28
CAPU = 32
CAPI = 32
CAPW = 4
NPOS = 4096
UR_DEV = 4096
IR_DEV = 2048
WR_DEV = 64
USERS = 65536
ITEMS = 32768
WEEKS = 1024
N_WIDE = 16
DEVICES = 128


def place_ends(values, own_key, smallest, high):
    spot = [jax.random.randint(jax.random.fold_in(own_key, axis), (), 0, length) for axis, length in enumerate(values.shape)]
    widest = values.shape.index(max(values.shape))
    neighbour = spot[:widest] + [(spot[widest] + 1) % values.shape[widest]] + spot[widest + 1:]
    return values.at[tuple(spot)].set(smallest).at[tuple(neighbour)].set(high)


def levels(own_key, shape, pieces, least, high):
    def one(position, blocks):
        steps = jax.random.uniform(jax.random.fold_in(jax.random.fold_in(own_key, 6), position), (blocks,), jnp.float32, least / len(pieces), high / len(pieces))
        return jnp.repeat(jnp.exp(steps), shape[position] // blocks).reshape((-1,) + (1,) * (len(shape) - position - 1))

    gain = one(*pieces[0])
    for cut in pieces[1:]:
        gain = gain * one(*cut)
    return gain


def length_profile(amount, total, limit, slope):
    portions = [(1 << 20) // math.isqrt(grade ** slope) + 1 for grade in range(2, amount + 1)]
    spare, given = total - limit - (amount - 1), [1] * (amount - 1)
    while spare > 0:
        candidates = [i for i in range(amount - 1) if given[i] < limit]
        mass, budget = sum([portions[i] for i in candidates]), spare
        for i in candidates:
            extra = min(limit - given[i], max(1, budget * portions[i] // mass), spare)
            given[i] = given[i] + extra
            spare = spare - extra
    return np.array([limit] + given)


def ragged_sizes(own_key, number_of, total, limit, skew):
    if number_of == 2:
        one = jax.random.randint(own_key, (), max(1, total - limit), min(limit, total - 1) + 1)
        return jnp.stack([one, total - one])
    lengths = jnp.asarray(length_profile(number_of, total, limit, skew), jnp.int32)
    pairs = (number_of - 1) // 2
    giver, taker = lengths[1:1 + 2 * pairs:2], lengths[2:2 + 2 * pairs:2]
    margin = jnp.minimum(giver - 1, limit - taker)
    moved = jax.random.randint(jax.random.fold_in(own_key, 1), (pairs,), 0, 1 << 20) % (margin + 1)
    lengths = lengths.at[1:1 + 2 * pairs:2].set(giver - moved).at[2:2 + 2 * pairs:2].set(taker + moved)
    return lengths[jax.random.permutation(jax.random.fold_in(own_key, 2), number_of)]


def centred(key, shape, deviation, most, split=(), held_as=jnp.bfloat16):
    drawn = deviation * jax.random.normal(key, shape, jnp.float32)
    if split:
        drawn = drawn * levels(key, shape, split, -0.22, 0.18)
    return jnp.clip(drawn, -most, most).astype(held_as)


def setup_inputs(seed: int = 0) -> dict:
    splits = jax.random.split(jax.random.key(seed), 13)
    user_table = centred(splits[0], (USERS, RANK), 0.5, 3.0, ((0, 16),))
    item_table = centred(splits[1], (ITEMS, RANK), 0.5, 3.0, ((0, 16),))
    week_table = centred(splits[2], (WEEKS, RANK), 0.5, 3.0, ((0, 16),))
    profile = centred(splits[3], (USERS, FEAT), 1.0, 6.0, ((0, 16), (1, 8)))
    feature_table = centred(splits[4], (FEAT, RANK), 0.0625, 0.375, ((0, 8),))
    user_req = place_ends(jax.random.randint(splits[5], (DEVICES, N_WIDE, CAPU), 0, UR_DEV), jax.random.fold_in(splits[5], 1), 0, UR_DEV - 1).astype(jnp.int32)
    item_req = place_ends(jax.random.randint(splits[6], (DEVICES, N_WIDE, CAPI), 0, IR_DEV), jax.random.fold_in(splits[6], 1), 0, IR_DEV - 1).astype(jnp.int32)
    week_req = place_ends(jax.random.randint(splits[7], (DEVICES, N_WIDE, CAPW), 0, WR_DEV), jax.random.fold_in(splits[7], 1), 0, WR_DEV - 1).astype(jnp.int32)
    user_counts = jax.vmap(lambda own: ragged_sizes(own, N_WIDE, BU, CAPU, 1))(jax.random.split(splits[8], DEVICES)).reshape((DEVICES, N_WIDE)).astype(jnp.int32)
    item_counts = jax.vmap(lambda own: ragged_sizes(own, N_WIDE, BI, CAPI, 1))(jax.random.split(splits[9], DEVICES)).reshape((DEVICES, N_WIDE)).astype(jnp.int32)
    week_counts = jax.vmap(lambda own: ragged_sizes(own, N_WIDE, BW, CAPW, 1))(jax.random.split(splits[10], DEVICES)).reshape((DEVICES, N_WIDE)).astype(jnp.int32)
    pos_cells = place_ends(jax.random.randint(splits[11], (DEVICES, NPOS), 0, BW * BU * BI), jax.random.fold_in(splits[11], 1), 0, (BW * BU * BI) - 1).astype(jnp.int32)
    return {"user_table": user_table, "item_table": item_table, "week_table": week_table, "profile": profile, "feature_table": feature_table, "user_req": user_req, "item_req": item_req, "week_req": week_req, "user_counts": user_counts, "item_counts": item_counts, "week_counts": week_counts, "pos_cells": pos_cells}


def compact_index(counts, cap, total):
    ends = jnp.cumsum(counts).astype(jnp.int32)
    starts = ends - counts
    place = jnp.arange(total, dtype=jnp.int32)
    owner = jnp.sum((ends[None, :] <= place[:, None]).astype(jnp.int32), axis=1)
    onehot = (owner[:, None] == jnp.arange(counts.shape[0], dtype=jnp.int32)[None, :]).astype(jnp.int32)
    first = jnp.sum(onehot * starts[None, :], axis=1)
    return (owner * cap + place - first).astype(jnp.int32)


def block_grads(user_rows, item_rows, week_rows, pos):
    nweek, nuser, nitem = week_rows.shape[0], user_rows.shape[0], item_rows.shape[0]
    user_f = user_rows.astype(jnp.float32)
    week_f = week_rows.astype(jnp.float32)
    item_f = item_rows.astype(jnp.float32)
    mixed = (user_f[None] * week_f[:, None]).astype(jnp.bfloat16)
    mixed_f = mixed.astype(jnp.float32)
    model = jnp.einsum("kir,jr->kij", mixed_f, item_f)
    cells = nweek * nuser * nitem
    cpos = jnp.zeros((cells,), jnp.float32).at[pos].set(1.0).reshape(nweek, nuser, nitem)
    resid = (jax.nn.sigmoid(model) - cpos).astype(jnp.bfloat16).astype(jnp.float32)
    partial_value = jnp.einsum("kij,jr->kir", resid, item_f)
    grad_u = jnp.sum(partial_value * week_f[:, None, :], axis=0)
    grad_w = jnp.sum(partial_value * user_f[None], axis=1)
    grad_v = jnp.einsum("kij,kir->jr", resid, mixed_f)
    return grad_u, grad_v, grad_w


def reference(user_table, item_table, week_table, profile, feature_table, user_req, item_req, week_req, user_counts, item_counts, week_counts, pos_cells):
    owners = jnp.arange(N_WIDE, dtype=jnp.int32)[:, None]

    def one_block(carry, device):
        acc_u, acc_v, acc_w = carry
        glob_u = (owners * UR_DEV + user_req[device]).reshape(-1)[compact_index(user_counts[device], CAPU, BU)]
        glob_v = (owners * IR_DEV + item_req[device]).reshape(-1)[compact_index(item_counts[device], CAPI, BI)]
        glob_w = (owners * WR_DEV + week_req[device]).reshape(-1)[compact_index(week_counts[device], CAPW, BW)]
        grad_u, grad_v, grad_w = block_grads(user_table[glob_u], item_table[glob_v], week_table[glob_w], pos_cells[device])
        return (acc_u.at[glob_u].add(grad_u), acc_v.at[glob_v].add(grad_v), acc_w.at[glob_w].add(grad_w)), None

    start = (jnp.zeros((USERS, RANK), jnp.float32), jnp.zeros((ITEMS, RANK), jnp.float32), jnp.zeros((WEEKS, RANK), jnp.float32))
    (acc_u, acc_v, acc_w), _ = lax.scan(one_block, start, jnp.arange(DEVICES, dtype=jnp.int32))

    slabs_u = user_table.reshape(N_WIDE, UR_DEV, RANK)
    slabs_x = profile.reshape(N_WIDE, UR_DEV, FEAT)

    def one_slab(acc_h, pair):
        slab_u, slab_x = pair
        model = jnp.dot(slab_u, feature_table.T, preferred_element_type=jnp.float32)
        resid = (model - slab_x.astype(jnp.float32)).astype(jnp.bfloat16)
        grad_u = 0.0625 * jnp.dot(resid, feature_table, preferred_element_type=jnp.float32)
        grad_h = 0.0625 * jnp.dot(resid.T, slab_u, preferred_element_type=jnp.float32)
        return acc_h + grad_h, grad_u

    grad_h, prof_u = lax.scan(one_slab, jnp.zeros((FEAT, RANK), jnp.float32), (slabs_u, slabs_x))
    grad_users = acc_u + prof_u.reshape(USERS, RANK)
    return grad_users, acc_v, acc_w, grad_h
```

```python
import functools

import jax
import jax.numpy as jnp
from jax import lax
from jax.experimental import pallas as pl
from jax.experimental.pallas import tpu as pltpu
from jax.sharding import PartitionSpec as P

RANK = 256
BU = 256
BI = 256
BW = 28
CAPU = 32
CAPI = 32
CAPW = 4
CAPX = 16
MSG = CAPU + CAPI + CAPX
GROUP = 4
HALF = BW // 2
MESH = pl.DeviceIdType.MESH
F32, BF16, I32, I16 = jnp.float32, jnp.bfloat16, jnp.int32, jnp.int16


def dot(a, b):
    return jnp.dot(a, b, preferred_element_type=F32)


def dot_nt(a, b):
    return lax.dot_general(a, b, (((1,), (1,)), ((), ())), preferred_element_type=F32)


def dot_tn(a, b):
    return lax.dot_general(a, b, (((0,), (0,)), ((), ())), preferred_element_type=F32)


def iota(shape, axis):
    return lax.broadcasted_iota(I32, shape, axis)


def flat_index(counts, owners, place, cap):
    flat, end = place, 0
    for o in range(owners):
        c = counts[0, o]
        end = end + c
        flat = flat + jnp.where(place >= end, cap - c, 0)
    return flat


def halves(q):
    high = jnp.round(q * (1.0 / 256.0))
    return high, q - 256.0 * high


def kernel(
    W,
    NY,
    utab,
    itab,
    wtab,
    prof,
    ftab,
    reqs,
    ucnt,
    icnt,
    wcnt,
    pos,
    out_u,
    out_i,
    out_w,
    out_f,
    uv,
    iv,
    wv,
    xv,
    fv,
    x2,
    f2,
    rq,
    hot,
    rowsend,
    rowbuf,
    gp,
    pring,
    feat,
    fsend,
    frecv,
    fall,
    pos_s,
    near,
    keep,
    cacc,
    bits,
    uf,
    wf,
    vb,
    vt,
    gu,
    gv,
    gw,
    msg,
    mbuf,
    sbuf,
    accu,
    acci,
    accw,
    load_sem,
    req_ss,
    req_rs,
    x_ss,
    x_rs,
    row_ss,
    row_rs,
    fr_ss,
    fr_rs,
    fa_ss,
    fa_rs,
    pr_ss,
    pr_rs,
    ms_ss,
    ms_rs,
    ring_ss,
    ring_rs,
    sib_ss,
    sib_rs,
):
    me = lax.axis_index("wide")
    nar = lax.axis_index("narrow")
    y, c = nar // 2, nar % 2
    step = 1 - 2 * c
    nxt = lax.rem(y + step + NY, NY) * 2 + c
    prv = lax.rem(y - step + NY, NY) * 2 + c
    sib = y * 2 + 1 - c
    UR, IR, WR = uv.shape[0], iv.shape[0], wv.shape[0]
    FD = fv.shape[0]
    US, IS, WS = UR // (2 * NY), IR // (2 * NY), WR // (2 * NY)
    FC = FD // W

    def wrap(a):
        return lax.rem(a + W, W)

    def rcopy(src, dst, ss, rs, dev):
        return pltpu.make_async_remote_copy(
            src_ref=src,
            dst_ref=dst,
            send_sem=ss,
            recv_sem=rs,
            device_id=dev,
            device_id_type=MESH,
        )

    def peers(fn):
        lax.fori_loop(1, W, lambda s, z: (fn(s), z)[1], 0)

    loads = [
        pltpu.make_async_copy(utab, uv, load_sem.at[0]),
        pltpu.make_async_copy(itab, iv, load_sem.at[1]),
        pltpu.make_async_copy(wtab, wv, load_sem.at[2]),
        pltpu.make_async_copy(ftab, fv, load_sem.at[3]),
        pltpu.make_async_copy(prof, xv, load_sem.at[4]),
    ]
    for cp in loads:
        cp.start()
    barrier = pltpu.get_barrier_semaphore()
    peers(
        lambda s: pl.semaphore_signal(
            barrier, inc=1, device_id={"wide": wrap(me + s)}, device_id_type=MESH
        )
    )
    for n in (nxt, prv, sib):
        pl.semaphore_signal(barrier, inc=1, device_id={"narrow": n}, device_id_type=MESH)
    pl.semaphore_wait(barrier, W - 1 + 3)

    def req_copy(s):
        return rcopy(
            reqs.at[wrap(me + s)],
            rq.at[s],
            req_ss.at[s],
            req_rs.at[s],
            {"wide": wrap(me + s)},
        )

    peers(lambda s: req_copy(s).start())
    rq[0] = reqs[me]

    def x_copy(q):
        row = pl.multiple_of((2 * q + 1 - c) * US, US)
        return rcopy(
            prof.at[pl.ds(row, US), :], x2.at[q], x_ss.at[q], x_rs.at[q], {"narrow": sib}
        )

    f_copy = rcopy(ftab, f2, x_ss.at[NY], x_rs.at[NY], {"narrow": sib})
    f_copy.start()
    for q in range(NY):
        x_copy(q).start()

    for cp in loads[:3]:
        cp.wait()
    peers(lambda s: req_copy(s).wait_recv())
    RT = jnp.swapaxes(rq[...].reshape(W * 8, 128), 0, 1)

    def row_copy(s):
        return rcopy(
            rowsend.at[s],
            rowbuf.at[me],
            row_ss.at[s],
            row_rs.at[s],
            {"wide": wrap(me - s)},
        )

    part = W // 2
    for m in range(2):
        slots = range(m * part, (m + 1) * part)
        for table, kind, cap, first in ((uv, 0, CAPU, 0), (iv, 1, CAPI, CAPU), (wv, 2, CAPX, CAPU + CAPI)):
            rows = table.shape[0]
            for a, s in enumerate(slots):
                col = jnp.broadcast_to(RT[0:cap, 8 * s + kind : 8 * s + kind + 1], (cap, rows))
                hot[a * cap : (a + 1) * cap, 0:rows] = jnp.where(
                    col == iota((cap, rows), 1), 1.0, 0.0
                ).astype(BF16)
            got = dot(hot[0 : part * cap, 0:rows], table[...]).astype(BF16)
            rowsend[m * part : (m + 1) * part, first : first + cap, :] = got.reshape(part, cap, RANK)
        for s in slots:
            if s > 0:
                row_copy(s).start()
    rowbuf[me] = rowsend[0]

    for cp in loads[3:]:
        cp.wait()
    feat[...] = jnp.zeros_like(feat)

    def resid(row, x, f):
        return (dot_nt(uv[pl.ds(row, US), :], f) - x.astype(F32)).astype(BF16)

    def own_rows(q, z):
        row = pl.multiple_of((2 * q + c) * US, US)
        r = resid(row, xv[pl.ds(row, US), :], fv[...])
        feat[...] += dot_tn(uv[pl.ds(row, US), :], r)
        gp[q] = 0.0625 * dot(r, fv[...])
        row = pl.multiple_of((2 * q + 1 - c) * US, US)
        r = resid(row, xv[pl.ds(row, US), :], fv[...])
        feat[...] += dot_tn(uv[pl.ds(row, US), :], r)
        return z

    lax.fori_loop(0, NY, own_rows, 0)
    fsend[...] = (0.0625 * jnp.swapaxes(feat[...], 0, 1)).reshape(W, FC, RANK)

    def fr_copy(s):
        return rcopy(
            fsend.at[wrap(me + s)],
            frecv.at[s],
            fr_ss.at[s],
            fr_rs.at[s],
            {"wide": wrap(me + s)},
        )

    peers(lambda s: fr_copy(s).start())
    frecv[0] = fsend[me]
    f_copy.wait_recv()
    for q in range(NY):
        x_copy(q).wait_recv()

    def sib_rows(q, z):
        row = pl.multiple_of((2 * q + c) * US, US)
        gp[q] += 0.0625 * dot(resid(row, x2[q], f2[...]), f2[...])
        return z

    lax.fori_loop(0, NY, sib_rows, 0)

    def pr_copy(h):
        src = gp.at[lax.rem(y - step + NY, NY)] if h == 0 else pring.at[h - 1]
        return rcopy(src, pring.at[h], pr_ss.at[h], pr_rs.at[h], {"narrow": nxt})

    def pr_hop(h):
        pr_copy(h - 1).wait_recv()
        q = lax.rem(y - (h + 1) * step + 2 * NY, NY)
        pring[h - 1] += gp[q]
        if h < NY - 1:
            pr_copy(h).start()

    pr_copy(0).start()

    for k in range(32):
        pos_s[k : k + 1, :] = pos[:, 128 * k : 128 * (k + 1)]
    big = 1 << 30
    near[...] = jnp.full(near.shape, big, I32)
    pt = jnp.swapaxes(
        jnp.concatenate([pos_s[...], jnp.zeros((96, 128), I32)], axis=0), 0, 1
    )
    for k in range(32):
        mb = jnp.broadcast_to(pt[:, k : k + 1], (128, 128))
        x = jnp.where(iota((128, 128), 0) < iota((128, 128), 1), mb ^ pos_s[k : k + 1, :], big)
        best = near[k]
        for t in range(16):
            best = jnp.minimum(best, x[8 * t : 8 * t + 8, :])
        near[k] = best

        def later(n, z, mb=mb):
            row = jnp.broadcast_to(pos_s[pl.ds(n, 1), :], (8, 128))
            best = near[n]
            for t in range(16):
                best = jnp.minimum(best, mb[8 * t : 8 * t + 8, :] ^ row)
            near[n] = best
            return z

        lax.fori_loop(k + 1, 32, later, 0)
    for k in range(32):
        keep[:, 128 * k : 128 * (k + 1)] = jnp.min(near[k].astype(F32), axis=0, keepdims=True)
    cacc[...] = jnp.zeros_like(cacc)

    def mark(n, z):
        at = pl.ds(pl.multiple_of(n * 512, 512), 512)
        p = pos[:, at]
        week, user, item = p >> 16, (p >> 8) & 255, p & 255
        late = week >= HALF
        bit = jnp.left_shift(jnp.ones_like(week), jnp.where(late, week - HALF, week))
        w = jnp.where(keep[:, at] > 0.5, bit.astype(F32), 0.0)
        row = iota((256, 512), 0)
        mine = row == user
        a0 = jnp.where(mine, jnp.where(late, 0.0, w), 0.0).astype(BF16)
        a1 = jnp.where(mine, jnp.where(late, w, 0.0), 0.0).astype(BF16)
        b = jnp.where(row == item, 1.0, 0.0).astype(BF16)
        cacc[...] += dot_nt(jnp.concatenate([a0, a1], axis=0), b)
        return z

    lax.fori_loop(0, pos.shape[1] // 512, mark, 0)
    bits[...] = cacc[0:BU, :].astype(I32) | (cacc[BU : 2 * BU, :].astype(I32) << HALF)

    def pick(counts, n, cap):
        flat = flat_index(counts, W, iota((n, 1), 0), cap)
        return jnp.where(flat == iota((n, W * cap), 1), 1.0, 0.0).astype(BF16)

    pu, pv, pw = pick(ucnt, BU, CAPU), pick(icnt, BI, CAPI), pick(wcnt, 32, CAPX)

    def row_wait(s):
        rcopy(
            rowsend.at[s],
            rowbuf.at[wrap(me + s)],
            row_ss.at[s],
            row_rs.at[s],
            {"wide": wrap(me - s)},
        ).wait_recv()

    peers(row_wait)
    uf[...] = dot(pu, rowbuf[:, 0:CAPU, :].reshape(W * CAPU, RANK))
    vf = dot(pv, rowbuf[:, CAPU : CAPU + CAPI, :].reshape(W * CAPI, RANK))
    wf[...] = dot(pw, rowbuf[:, CAPU + CAPI : MSG, :].reshape(W * CAPX, RANK))
    vb[...] = vf.astype(BF16)
    vt[...] = jnp.swapaxes(vf, 0, 1).astype(BF16)
    gu[...] = jnp.zeros_like(gu)
    gv[...] = jnp.zeros_like(gv)
    gw[...] = jnp.zeros_like(gw)

    def week(k):
        w = wf[pl.ds(k, 1), :]
        uw = (uf[...] * w).astype(BF16)
        m = dot(uw, vt[...])
        hit = ((bits[...] >> k) & 1).astype(F32)
        g = (0.5 * jnp.tanh(0.5 * m) + (0.5 - hit)).astype(BF16)
        q = dot(g, vb[...])
        gu[...] += q * w
        gw[pl.ds(k, 1), :] = jnp.sum(q * uf[...], axis=0, keepdims=True)
        gv[...] += dot_tn(g, uw)

    def weeks(lo, hi):
        def two(k, z):
            week(2 * k)
            week(2 * k + 1)
            return z

        lax.fori_loop(lo // 2, hi // 2, two, 0)

    weeks(0, 10)
    pr_hop(1)

    peers(lambda s: fr_copy(s).wait_recv())
    total = frecv[0]
    for s in range(1, W):
        total = total + frecv[s]
    fall[me] = total

    def fa_copy(s):
        return rcopy(fall.at[me], fall.at[me], fa_ss.at[s], fa_rs.at[s], {"wide": wrap(me + s)})

    peers(lambda s: fa_copy(s).start())
    weeks(10, 20)
    pr_hop(2)
    weeks(20, BW)

    def encode(g, counts, cap):
        n = g.shape[0]
        top = jnp.maximum(jnp.max(jnp.abs(g), axis=1, keepdims=True), 2.0**-100)
        e = jnp.ceil(jnp.log2(top)) - 15.0
        q = jnp.clip(jnp.round(g * jnp.exp2(-e)), -32767.0, 32767.0)
        high, low = halves(q)
        rhs = jnp.concatenate([high, low, jnp.broadcast_to(e, (n, 128))], axis=1).astype(BF16)
        flat = flat_index(counts, W, iota((1, n), 1), cap)
        sel = jnp.where(flat == iota((W * cap, n), 0), 1.0, 0.0).astype(BF16)
        got = dot(sel, rhs)
        code = (256.0 * got[:, 0:RANK] + got[:, RANK : 2 * RANK]).astype(I32)
        es = got[:, 2 * RANK :].reshape(W, cap, 128)
        es = jnp.where(iota((W, cap, 128), 1) == iota((W, cap, 128), 2) % cap, es, 0.0)
        es = jnp.sum(es, axis=1, keepdims=True).astype(I32)
        return code.reshape(W, cap, RANK), es

    ucode, ue = encode(gu[...], ucnt, CAPU)
    msg[:, 0:CAPU, :] = ucode.astype(I16)
    vcode, ve = encode(gv[...], icnt, CAPI)
    msg[:, CAPU : CAPU + CAPI, :] = vcode.astype(I16)
    wcode, we = encode(gw[...], wcnt, CAPX)
    shape = (W, CAPX, RANK)
    none = jnp.zeros_like(we)
    tail = wcode
    for r, left, right in (
        (8, reqs[:, 0:1, :], reqs[:, 1:2, :]),
        (9, reqs[:, 2:3, :], none),
        (10, ue, ve),
        (11, we, none),
    ):
        line = jnp.broadcast_to(jnp.concatenate([left, right], axis=2), shape)
        tail = jnp.where(iota(shape, 1) == r, line, tail)
    msg[:, CAPU + CAPI : MSG, :] = tail.astype(I16)

    def ms_copy(s):
        return rcopy(
            msg.at[wrap(me + s)],
            mbuf.at[0, s],
            ms_ss.at[s],
            ms_rs.at[s],
            {"wide": wrap(me + s)},
        )

    peers(lambda s: ms_copy(s).start())
    mbuf[0, 0] = msg[me]

    groups = W // GROUP

    def span(g):
        return pl.ds(g * GROUP, GROUP)

    def ring_copy(h, g):
        return rcopy(
            mbuf.at[h, span(g)],
            mbuf.at[h + 1, span(g)],
            ring_ss.at[h, g],
            ring_rs.at[h, g],
            {"narrow": nxt},
        )

    def sib_copy(h, g):
        return rcopy(
            mbuf.at[h, span(g)],
            sbuf.at[h, span(g)],
            sib_ss.at[h, g],
            sib_rs.at[h, g],
            {"narrow": sib},
        )

    share = nar
    accu[...] = jnp.zeros_like(accu)
    acci[...] = jnp.zeros_like(acci)
    accw[...] = jnp.zeros_like(accw)

    def lanes(tail_rows, r, first, cap):
        each = 128 // cap
        pieces = []
        for p in range(W // each):
            piece = jnp.zeros((1, 128), F32)
            for a in range(each):
                line = tail_rows[p * each + a, r : r + 1, first : first + 128]
                piece = jnp.where(iota((1, 128), 1) // cap == a, line, piece)
            pieces.append(piece)
        return jnp.concatenate(pieces, axis=1)

    def add_rows(buf, h):
        tail_rows = buf[h, :, CAPU + CAPI : MSG, :].astype(I32).astype(F32)
        for acc, kind, lo, cap, size in (
            (accu, 0, 0, CAPU, US),
            (acci, 1, CAPU, CAPI, IS),
            (accw, 2, CAPU + CAPI, CAPX, WS),
        ):
            r, first = (8, 128 * kind) if kind < 2 else (9, 0)
            ids = lanes(tail_rows, r, first, cap)
            scale = jnp.exp2(lanes(tail_rows, r + 2, first, cap))
            rows = acc.shape[0]
            place = (iota((rows, W * cap), 0) + share * size).astype(F32)
            sel = jnp.where(ids == place, jnp.broadcast_to(scale, place.shape), 0.0).astype(BF16)
            q = buf[h, :, lo : lo + cap, :].astype(I32).astype(F32)
            if kind == 2:
                q = jnp.where(iota(q.shape, 1) < CAPW, q, 0.0)
            high, low = halves(q.reshape(W * cap, RANK))
            acc[...] += dot(sel, jnp.concatenate([high, low], axis=1).astype(BF16))

    for g in range(groups):
        for s in range(g * GROUP, (g + 1) * GROUP):
            if s > 0:
                ms_copy(s).wait_recv()
        ring_copy(0, g).start()
        sib_copy(0, g).start()
    pr_hop(3)

    def fa_wait(s):
        rcopy(
            fall.at[me],
            fall.at[wrap(me - s)],
            fa_ss.at[s],
            fa_rs.at[s],
            {"wide": wrap(me + s)},
        ).wait_recv()

    peers(fa_wait)
    out_f[...] = fall[...].reshape(FD, RANK)
    add_rows(mbuf, 0)
    for h in range(1, NY):
        for g in range(groups):
            ring_copy(h - 1, g).wait_recv()
            if h < NY - 1:
                ring_copy(h, g).start()
            sib_copy(h, g).start()
        for g in range(groups):
            sib_copy(h - 1, g).wait_recv()
        add_rows(sbuf, h - 1)
        add_rows(mbuf, h)
    for g in range(groups):
        sib_copy(NY - 1, g).wait_recv()
    add_rows(sbuf, NY - 1)

    out_u[...] = 256.0 * accu[:, 0:RANK] + accu[:, RANK:] + pring[NY - 2]
    out_i[...] = 256.0 * acci[:, 0:RANK] + acci[:, RANK:]
    out_w[...] = 256.0 * accw[0:WS, 0:RANK] + accw[0:WS, RANK:]

    def sent(s):
        req_copy(s).wait_send()
        row_copy(s).wait_send()
        fr_copy(s).wait_send()
        fa_copy(s).wait_send()
        ms_copy(s).wait_send()

    peers(sent)
    f_copy.wait_send()
    for q in range(NY):
        x_copy(q).wait_send()
    for h in range(NY - 1):
        pr_copy(h).wait_send()
        for g in range(groups):
            ring_copy(h, g).wait_send()
    for h in range(NY):
        for g in range(groups):
            sib_copy(h, g).wait_send()


def local(
    W,
    NY,
    user_table,
    item_table,
    week_table,
    profile,
    feature_table,
    user_req,
    item_req,
    week_req,
    user_counts,
    item_counts,
    week_counts,
    pos_cells,
):
    lines = jnp.stack(
        [
            jnp.tile(user_req[0], (1, 128 // CAPU)),
            jnp.tile(item_req[0], (1, 128 // CAPI)),
            jnp.tile(jnp.pad(week_req[0], ((0, 0), (0, CAPX - CAPW))), (1, 128 // CAPX)),
        ],
        axis=1,
    )
    reqs = jnp.pad(lines, ((0, 0), (0, 5), (0, 0)))
    UR, IR, WR = user_table.shape[0], item_table.shape[0], week_table.shape[0]
    FD = feature_table.shape[0]
    US, IS, WS = UR // (2 * NY), IR // (2 * NY), WR // (2 * NY)
    FC = FD // W
    groups = W // GROUP
    V, D = pltpu.VMEM, pltpu.SemaphoreType.DMA
    anywhere = pl.BlockSpec(memory_space=pl.ANY)
    vmem = pl.BlockSpec(memory_space=pltpu.VMEM)
    smem = pl.BlockSpec(memory_space=pltpu.SMEM)
    return pl.pallas_call(
        functools.partial(kernel, W, NY),
        out_shape=(
            jax.ShapeDtypeStruct((US, RANK), F32),
            jax.ShapeDtypeStruct((IS, RANK), F32),
            jax.ShapeDtypeStruct((WS, RANK), F32),
            jax.ShapeDtypeStruct((FD, RANK), F32),
        ),
        in_specs=[anywhere] * 5 + [vmem] + [smem] * 3 + [vmem],
        out_specs=(vmem, vmem, vmem, vmem),
        scratch_shapes=[
            V((UR, RANK), BF16),
            V((IR, RANK), BF16),
            V((WR, RANK), BF16),
            V((UR, FD), BF16),
            V((FD, RANK), BF16),
            V((NY, US, FD), BF16),
            V((FD, RANK), BF16),
            V((W, 8, 128), I32),
            V((W // 2 * CAPU, UR), BF16),
            V((W, MSG, RANK), BF16),
            V((W, MSG, RANK), BF16),
            V((NY, US, RANK), F32),
            V((NY - 1, US, RANK), F32),
            V((RANK, FD), F32),
            V((W, FC, RANK), F32),
            V((W, FC, RANK), F32),
            V((W, FC, RANK), F32),
            V((32, 128), I32),
            V((32, 8, 128), I32),
            V((1, pos_cells.shape[1]), F32),
            V((2 * BU, BI), F32),
            V((BU, BI), I32),
            V((BU, RANK), F32),
            V((32, RANK), F32),
            V((BI, RANK), BF16),
            V((RANK, BI), BF16),
            V((BU, RANK), F32),
            V((BI, RANK), F32),
            V((32, RANK), F32),
            V((W, MSG, RANK), I16),
            V((NY, W, MSG, RANK), I16),
            V((NY, W, MSG, RANK), I16),
            V((US, 2 * RANK), F32),
            V((IS, 2 * RANK), F32),
            V((16, 2 * RANK), F32),
            D((5,)),
            D((W,)),
            D((W,)),
            D((NY + 1,)),
            D((NY + 1,)),
            D((W,)),
            D((W,)),
            D((W,)),
            D((W,)),
            D((W,)),
            D((W,)),
            D((NY - 1,)),
            D((NY - 1,)),
            D((W,)),
            D((W,)),
            D((NY - 1, groups)),
            D((NY - 1, groups)),
            D((NY, groups)),
            D((NY, groups)),
        ],
        compiler_params=pltpu.CompilerParams(
            collective_id=0, has_side_effects=True, vmem_limit_bytes=56 << 20
        ),
    )(
        user_table,
        item_table,
        week_table,
        profile,
        feature_table,
        reqs,
        user_counts,
        item_counts,
        week_counts,
        pos_cells,
    )


def solution(mesh):
    W, NY = mesh.shape["wide"], mesh.shape["narrow"] // 2
    both = ("wide", "narrow")
    return jax.shard_map(
        functools.partial(local, W, NY),
        mesh=mesh,
        in_specs=(
            P("wide", None),
            P("wide", None),
            P("wide", None),
            P("wide", "narrow"),
            P("narrow", None),
            P(both, None, None),
            P(both, None, None),
            P(both, None, None),
            P(both, None),
            P(both, None),
            P(both, None),
            P(both, None),
        ),
        out_specs=(P(both, None), P(both, None), P(both, None), P("narrow", None)),
        check_vma=False,
    )
```

```python
import functools

import jax
import jax.numpy as jnp
from jax import lax
from jax.experimental import pallas as pl
from jax.experimental.pallas import tpu as pltpu
from jax.sharding import PartitionSpec as P

RANK = 256
BU = 256
BI = 256
BW = 28
CAPU = 32
CAPI = 32
CAPW = 4
CAPX = 16
MSG = CAPU + CAPI + CAPX
GROUP = 4
GROUPS = (0, 1, 3, 2)
FIELDS = 12
BLOCK = 4
THIRD = 3
PAIR = 2
SIDE = 4
ORDER = (1, 4, 3, 12, 5, 15, 7, 13, 2, 8, 9, 14, 11, 6, 10)
MESH = pl.DeviceIdType.MESH
F32, BF16, I32, I16 = jnp.float32, jnp.bfloat16, jnp.int32, jnp.int16


def dot(a, b):
    return jnp.dot(a, b, preferred_element_type=F32)


def dot_nt(a, b):
    return lax.dot_general(a, b, (((1,), (1,)), ((), ())), preferred_element_type=F32)


def dot_tn(a, b):
    return lax.dot_general(a, b, (((0,), (0,)), ((), ())), preferred_element_type=F32)


def iota(shape, axis):
    return lax.broadcasted_iota(I32, shape, axis)


def flat_index(counts, owners, place, cap):
    flat, end = place, 0
    for o in range(owners):
        c = counts[0, o]
        end = end + c
        flat = flat + jnp.where(place >= end, cap - c, 0)
    return flat


def halves(q):
    high = jnp.round(q * (1.0 / 256.0))
    return high, q - 256.0 * high


def exponent(top):
    return jnp.ceil(jnp.log2(jnp.maximum(top, 2.0**-100))) - 15.0


def quantize(x, e):
    return jnp.clip(jnp.round(x * jnp.exp2(-e)), -32767.0, 32767.0)


def kernel(
    W,
    NY,
    utab,
    itab,
    wtab,
    prof,
    ftab,
    ureq,
    ireq,
    wreq,
    ucnt,
    icnt,
    wcnt,
    pos,
    out_u,
    out_i,
    out_w,
    out_f,
    uv,
    iv,
    wv,
    xv,
    fv,
    x2,
    f2,
    reqs,
    rq,
    hot,
    rowsend,
    rowbuf,
    gp,
    prsend,
    pring,
    feat,
    fsend,
    frecv,
    fall,
    pos_s,
    near,
    keep,
    spread,
    cacc,
    bits,
    uf,
    wf,
    vb,
    vt,
    gu,
    gv,
    gw,
    uw0,
    uw1,
    mm0,
    mm1,
    gg0,
    gg1,
    msg,
    mbuf,
    sbuf,
    accu,
    acci,
    accw,
    load_sem,
    req_ss,
    req_rs,
    x_ss,
    x_rs,
    row_ss,
    row_rs,
    fr_ss,
    fr_rs,
    fa_ss,
    fa_rs,
    pr_ss,
    pr_rs,
    ms_ss,
    ms_rs,
    ring_ss,
    ring_rs,
    sib_ss,
    sib_rs,
):
    me = lax.axis_index("wide")
    nar = lax.axis_index("narrow")
    y, c = nar // 2, nar % 2
    step = 1 - 2 * c
    nxt = lax.rem(y + step + NY, NY) * 2 + c
    prv = lax.rem(y - step + NY, NY) * 2 + c
    sib = y * 2 + 1 - c
    UR, IR, WR = uv.shape[0], iv.shape[0], wv.shape[0]
    FD = fv.shape[0]
    US, IS, WS = UR // (2 * NY), IR // (2 * NY), WR // (2 * NY)
    FC = FD // W

    X, Z = me // SIDE, lax.rem(me, SIDE)

    def to(s):
        return lax.rem(X + s // SIDE, SIDE) * SIDE + lax.rem(Z + s % SIDE, SIDE)

    def frm(s):
        return lax.rem(X + SIDE - s // SIDE, SIDE) * SIDE + lax.rem(Z + SIDE - s % SIDE, SIDE)

    def rcopy(src, dst, ss, rs, dev):
        return pltpu.make_async_remote_copy(
            src_ref=src,
            dst_ref=dst,
            send_sem=ss,
            recv_sem=rs,
            device_id=dev,
            device_id_type=MESH,
        )

    def peers(fn):
        for s in ORDER:
            fn(s)

    leave, pend = [], {}

    loads = [
        pltpu.make_async_copy(utab, uv, load_sem.at[0]),
        pltpu.make_async_copy(itab, iv, load_sem.at[1]),
        pltpu.make_async_copy(wtab, wv, load_sem.at[2]),
        pltpu.make_async_copy(ftab, fv, load_sem.at[3]),
        pltpu.make_async_copy(prof, xv, load_sem.at[4]),
    ]
    for cp in loads:
        cp.start()
    pend["tables"] = lambda: [cp.wait() for cp in loads[:3]]
    pend["profile"] = lambda: [cp.wait() for cp in loads[3:]]
    barrier = pltpu.get_barrier_semaphore()
    peers(
        lambda s: pl.semaphore_signal(
            barrier, inc=1, device_id={"wide": to(s)}, device_id_type=MESH
        )
    )
    for n in (nxt, prv, sib):
        pl.semaphore_signal(barrier, inc=1, device_id={"narrow": n}, device_id_type=MESH)
    for kind, ids in ((0, ureq[...]), (1, ireq[...])):
        line = jnp.concatenate([ids] * (128 // ids.shape[1]), axis=1)
        for o in range(W):
            reqs[o, kind : kind + 1, :] = line[o : o + 1, :]
    used = jnp.concatenate([wreq[...], jnp.zeros((CAPX - CAPW, W), I32)], axis=0)
    used = jnp.concatenate([used] * (128 // CAPX), axis=0)
    used = jnp.swapaxes(jnp.concatenate([used] * (128 // W), axis=1), 0, 1)
    for o in range(W):
        reqs[o, 2:3, :] = used[o : o + 1, :]
        reqs[o, 3:8, :] = jnp.zeros((5, 128), I32)
    pl.semaphore_wait(barrier, W - 1 + 3)

    def req_copy(s):
        return rcopy(
            reqs.at[to(s)],
            rq.at[s],
            req_ss.at[s],
            req_rs.at[s],
            {"wide": to(s)},
        )

    peers(lambda s: req_copy(s).start())
    rq[0] = reqs[me]
    leave.append(lambda: peers(lambda s: req_copy(s).wait_send()))
    pend["rq"] = lambda: peers(lambda s: req_copy(s).wait_recv())

    def x_copy(q):
        row = pl.multiple_of((2 * q + 1 - c) * US, US)
        return rcopy(
            prof.at[pl.ds(row, US), :], x2.at[q], x_ss.at[q], x_rs.at[q], {"narrow": sib}
        )

    f_copy = rcopy(ftab, f2, x_ss.at[NY], x_rs.at[NY], {"narrow": sib})
    f_copy.start()
    for q in range(NY):
        x_copy(q).start()

    def x_wait():
        f_copy.wait_recv()
        for q in range(NY):
            x_copy(q).wait_recv()

    def x_sent():
        f_copy.wait_send()
        for q in range(NY):
            x_copy(q).wait_send()

    pend["x"] = x_wait
    leave.append(x_sent)

    big = 1 << 30

    def least(xs):
        while len(xs) > 1:
            xs = [jnp.minimum(a, b) for a, b in zip(xs[::2], xs[1::2])]
        return xs[0]

    lines = pos.shape[1] // 128
    for k in range(lines):
        pos_s[k : k + 1, :] = pos[:, 128 * k : 128 * (k + 1)]
    near[...] = jnp.full(near.shape, big, I32)
    pt = jnp.swapaxes(
        jnp.concatenate([pos_s[...], jnp.zeros((128 - lines, 128), I32)], axis=0), 0, 1
    )
    for k in range(lines):
        spread[k] = jnp.broadcast_to(pt[:, k : k + 1], (128, 128))

    def compare(k, block, masked):
        for a in range(BLOCK):
            n = block * BLOCK + a
            row = jnp.broadcast_to(pos_s[pl.ds(n, 1), :], (8, 128))
            xs = []
            for t in range(16):
                x = spread[k, 8 * t : 8 * t + 8, :] ^ row
                if masked:
                    first = k * 128 + 8 * t + iota((8, 128), 0)
                    x = jnp.where(first < n * 128 + iota((8, 128), 1), x, big)
                xs.append(x)
            near[n] = jnp.minimum(near[n], least(xs))

    def column(k, z):
        own = k // BLOCK
        stop = jnp.minimum((own // THIRD + 1) * THIRD, lines // BLOCK)
        compare(k, own, True)
        lax.fori_loop(own + 1, stop, lambda b, y: (compare(k, b, False), y)[1], 0)
        return z

    lax.fori_loop(0, lines, column, 0)
    for k in range(lines):
        keep[:, 128 * k : 128 * (k + 1)] = jnp.min(near[k].astype(F32), axis=0, keepdims=True)
    pend.pop("tables")()
    pend.pop("rq")()
    RT = jnp.swapaxes(rq[...].reshape(W * 8, 128), 0, 1)

    def row_copy(s):
        return rcopy(
            rowsend.at[s],
            rowbuf.at[me],
            row_ss.at[s],
            row_rs.at[s],
            {"wide": frm(s)},
        )

    part = W // 2
    for m in range(2):
        slots = range(m * part, (m + 1) * part)
        for table, kind, cap, first in ((uv, 0, CAPU, 0), (iv, 1, CAPI, CAPU), (wv, 2, CAPX, CAPU + CAPI)):
            rows = table.shape[0]
            for a, s in enumerate(slots):
                col = jnp.broadcast_to(RT[0:cap, 8 * s + kind : 8 * s + kind + 1], (cap, rows))
                hot[a * cap : (a + 1) * cap, 0:rows] = jnp.where(
                    col == iota((cap, rows), 1), 1.0, 0.0
                ).astype(BF16)
            got = dot(hot[0 : part * cap, 0:rows], table[...]).astype(BF16)
            rowsend[m * part : (m + 1) * part, first : first + cap, :] = got.reshape(part, cap, RANK)
        for s in ORDER:
            if s in slots:
                row_copy(s).start()
    rowbuf[me] = rowsend[0]

    def row_wait(s):
        rcopy(
            rowsend.at[s],
            rowbuf.at[to(s)],
            row_ss.at[s],
            row_rs.at[s],
            {"wide": frm(s)},
        ).wait_recv()

    leave.append(lambda: peers(lambda s: row_copy(s).wait_send()))
    pend["row"] = lambda: peers(row_wait)

    pend.pop("profile")()
    feat[...] = jnp.zeros_like(feat)

    def resid(row, x, f):
        return (dot_nt(uv[pl.ds(row, US), :], f) - x.astype(F32)).astype(BF16)

    def own_rows(q, z):
        row = pl.multiple_of((2 * q + c) * US, US)
        r = resid(row, xv[pl.ds(row, US), :], fv[...])
        feat[...] += dot_tn(uv[pl.ds(row, US), :], r)
        gp[q] = 0.0625 * dot(r, fv[...])
        row = pl.multiple_of((2 * q + 1 - c) * US, US)
        r = resid(row, xv[pl.ds(row, US), :], fv[...])
        feat[...] += dot_tn(uv[pl.ds(row, US), :], r)
        return z

    lax.fori_loop(0, NY, own_rows, 0)
    fsend[...] = (0.0625 * jnp.swapaxes(feat[...], 0, 1)).reshape(W, FC, RANK)

    def fr_copy(s):
        return rcopy(
            fsend.at[to(s)],
            frecv.at[s],
            fr_ss.at[s],
            fr_rs.at[s],
            {"wide": to(s)},
        )

    peers(lambda s: fr_copy(s).start())
    frecv[0] = fsend[me]
    leave.append(lambda: peers(lambda s: fr_copy(s).wait_send()))
    pend["fr"] = lambda: peers(lambda s: fr_copy(s).wait_recv())
    pend.pop("x")()

    def sib_rows(q, z):
        row = pl.multiple_of((2 * q + c) * US, US)
        gp[q] += 0.0625 * dot(resid(row, x2[q], f2[...]), f2[...])
        return z

    lax.fori_loop(0, NY, sib_rows, 0)

    def pr_copy(h):
        return rcopy(prsend.at[h], pring.at[h], pr_ss.at[h], pr_rs.at[h], {"narrow": nxt})

    def pr_start(h, x):
        e = exponent(jnp.max(jnp.abs(x), axis=0, keepdims=True))
        prsend[h, 0:US, :] = quantize(x, e).astype(I32).astype(I16)
        prsend[h, US:, :] = jnp.broadcast_to(e, (16, RANK)).astype(I32).astype(I16)
        pr_copy(h).start()
        leave.append(lambda: pr_copy(h).wait_send())
        pend["pr"] = lambda: pr_copy(h).wait_recv()

    def pr_hop(h):
        pend.pop("pr")()
        q = lax.rem(y - (h + 1) * step + 2 * NY, NY)
        e = pring[h - 1, US:, :].astype(I32).astype(F32)[0:1, :]
        x = pring[h - 1, 0:US, :].astype(I32).astype(F32) * jnp.exp2(e) + gp[q]
        if h < NY - 1:
            pr_start(h, x)
        else:
            gp[y] = x

    pr_start(0, gp[lax.rem(y - step + NY, NY)])

    cacc[...] = jnp.zeros_like(cacc)

    def mark(n, z):
        at = pl.ds(pl.multiple_of(n * 512, 512), 512)
        p = pos[:, at]
        week, user, item = p >> 16, (p >> 8) & 255, p & 255
        part = week // FIELDS
        bit = jnp.left_shift(jnp.ones_like(week), 2 * (week - FIELDS * part))
        w = jnp.where(keep[:, at] > 0.5, bit.astype(F32), 0.0)
        row = iota((256, 512), 0)
        mine = jnp.where(row == user, 1.0, 0.0).astype(BF16)
        a = [mine * jnp.where(part == f, w, 0.0).astype(BF16) for f in range(3)]
        b = jnp.where(row == item, 1.0, 0.0).astype(BF16)
        cacc[...] += dot_nt(jnp.concatenate(a, axis=0), b)
        return z

    lax.fori_loop(0, pos.shape[1] // 512, mark, 0)

    def present(f):
        n = cacc[f * BU : (f + 1) * BU, :].astype(I32)
        return (n | (n >> 1)) & 0x555555

    bits[...] = present(0) | (present(1) << 1) | (present(2) << (2 * FIELDS))

    def pick(counts, n, cap):
        flat = flat_index(counts, W, iota((n, 1), 0), cap)
        return jnp.where(flat == iota((n, W * cap), 1), 1.0, 0.0).astype(BF16)

    pu, pv, pw = pick(ucnt, BU, CAPU), pick(icnt, BI, CAPI), pick(wcnt, 32, CAPX)

    pend.pop("row")()
    uf[...] = dot(pu, rowbuf[:, 0:CAPU, :].reshape(W * CAPU, RANK))
    vf = dot(pv, rowbuf[:, CAPU : CAPU + CAPI, :].reshape(W * CAPI, RANK))
    wf[...] = dot(pw, rowbuf[:, CAPU + CAPI : MSG, :].reshape(W * CAPX, RANK))
    vb[...] = (0.5 * vf).astype(BF16)
    vt[...] = (0.5 * jnp.swapaxes(vf, 0, 1)).astype(BF16)
    gu[...] = jnp.zeros_like(gu)
    gv[...] = jnp.zeros_like(gv)
    gw[...] = jnp.zeros_like(gw)

    def lead(k, uw, mm):
        for a in range(PAIR):
            uw[BU * a : BU * (a + 1), :] = (uf[...] * wf[pl.ds(k + a, 1), :]).astype(BF16)
        mm[...] = dot(uw[...], vt[...])

    def work(k, uw, mm, gg):
        place = jnp.where(k < FIELDS, 2 * k, jnp.where(k < 2 * FIELDS, 2 * (k - FIELDS) + 1, 2 * (k - FIELDS)))
        hits = bits[...] >> place
        for a in range(PAIR):
            sign = jnp.where((hits & (1 << (2 * a))) != 0, -1.0, 1.0)
            at = slice(BU * a, BU * (a + 1))
            gg[at, :] = (jnp.tanh(mm[at, :]) + sign).astype(BF16)
        q = dot(gg[...], vb[...])
        total = gu[...]
        for a in range(PAIR):
            w, qa = wf[pl.ds(k + a, 1), :], q[BU * a : BU * (a + 1), :]
            total = total + qa * w
            gw[pl.ds(k + a, 1), :] = jnp.sum(qa * uf[...], axis=0, keepdims=True)
        gu[...] = total
        gv[...] += dot_tn(gg[...], uw[...])

    def weeks(lo, hi):
        def both(n, z):
            k = 2 * PAIR * n
            lead(k + PAIR, uw1, mm1)
            work(k, uw0, mm0, gg0)
            lead(k + 2 * PAIR, uw0, mm0)
            work(k + PAIR, uw1, mm1, gg1)
            return z

        lax.fori_loop(lo // (2 * PAIR), hi // (2 * PAIR), both, 0)

    lead(0, uw0, mm0)
    weeks(0, 12)
    pr_hop(1)

    pend.pop("fr")()
    total = frecv[0]
    for s in range(1, W):
        total = total + frecv[s]
    fall[me] = total

    def fa_copy(s):
        return rcopy(fall.at[me], fall.at[me], fa_ss.at[s], fa_rs.at[s], {"wide": to(s)})

    peers(lambda s: fa_copy(s).start())

    def fa_wait(s):
        rcopy(
            fall.at[me],
            fall.at[frm(s)],
            fa_ss.at[s],
            fa_rs.at[s],
            {"wide": to(s)},
        ).wait_recv()

    leave.append(lambda: peers(lambda s: fa_copy(s).wait_send()))
    pend["fa"] = lambda: peers(fa_wait)
    weeks(12, BW)
    pr_hop(2)

    def encode(g, counts, cap):
        n = g.shape[0]
        e = exponent(jnp.max(jnp.abs(g), axis=1, keepdims=True))
        high, low = halves(quantize(g, e))
        rhs = jnp.concatenate([high, low, jnp.broadcast_to(e, (n, 128))], axis=1).astype(BF16)
        flat = flat_index(counts, W, iota((1, n), 1), cap)
        sel = jnp.where(flat == iota((W * cap, n), 0), 1.0, 0.0).astype(BF16)
        got = dot(sel, rhs)
        code = (256.0 * got[:, 0:RANK] + got[:, RANK : 2 * RANK]).astype(I32)
        es = got[:, 2 * RANK :].reshape(W, cap, 128)
        es = jnp.where(iota((W, cap, 128), 1) == iota((W, cap, 128), 2) % cap, es, 0.0)
        es = jnp.sum(es, axis=1, keepdims=True).astype(I32)
        return code.reshape(W, cap, RANK), es

    ucode, ue = encode(gu[...], ucnt, CAPU)
    msg[:, 0:CAPU, :] = ucode.astype(I16)
    vcode, ve = encode(0.5 * gv[...], icnt, CAPI)
    msg[:, CAPU : CAPU + CAPI, :] = vcode.astype(I16)
    wcode, we = encode(gw[...], wcnt, CAPX)
    shape = (W, CAPX, RANK)
    none = jnp.zeros_like(we)
    tail = wcode
    for r, left, right in (
        (8, reqs[:, 0:1, :], reqs[:, 1:2, :]),
        (9, reqs[:, 2:3, :], none),
        (10, ue, ve),
        (11, we, none),
    ):
        line = jnp.broadcast_to(jnp.concatenate([left, right], axis=2), shape)
        tail = jnp.where(iota(shape, 1) == r, line, tail)
    msg[:, CAPU + CAPI : MSG, :] = tail.astype(I16)

    def ms_copy(s):
        return rcopy(
            msg.at[to(s)],
            mbuf.at[0, s],
            ms_ss.at[s],
            ms_rs.at[s],
            {"wide": to(s)},
        )

    peers(lambda s: ms_copy(s).start())
    mbuf[0, 0] = msg[me]
    leave.append(lambda: peers(lambda s: ms_copy(s).wait_send()))
    pend["ms"] = lambda: peers(lambda s: ms_copy(s).wait_recv())

    groups = W // GROUP

    def span(g):
        return pl.ds(g * GROUP, GROUP)

    def ring_copy(h, g):
        return rcopy(
            mbuf.at[h, span(g)],
            mbuf.at[h + 1, span(g)],
            ring_ss.at[h, g],
            ring_rs.at[h, g],
            {"narrow": nxt},
        )

    def sib_copy(h, g):
        return rcopy(
            mbuf.at[h, span(g)],
            sbuf.at[h, span(g)],
            sib_ss.at[h, g],
            sib_rs.at[h, g],
            {"narrow": sib},
        )

    share = nar
    accu[...] = jnp.zeros_like(accu)
    acci[...] = jnp.zeros_like(acci)
    accw[...] = jnp.zeros_like(accw)

    def lanes(tail_rows, r, first, cap):
        each = 128 // cap
        pieces = []
        for p in range(W // each):
            piece = jnp.zeros((1, 128), F32)
            for a in range(each):
                line = tail_rows[p * each + a, r : r + 1, first : first + 128]
                piece = jnp.where(iota((1, 128), 1) // cap == a, line, piece)
            pieces.append(piece)
        return jnp.concatenate(pieces, axis=1)

    def add_rows(buf, h):
        tail_rows = buf[h, :, CAPU + CAPI : MSG, :].astype(I32).astype(F32)
        for acc, kind, lo, cap, size in (
            (accu, 0, 0, CAPU, US),
            (acci, 1, CAPU, CAPI, IS),
            (accw, 2, CAPU + CAPI, CAPX, WS),
        ):
            r, first = (8, 128 * kind) if kind < 2 else (9, 0)
            ids = lanes(tail_rows, r, first, cap)
            scale = jnp.exp2(lanes(tail_rows, r + 2, first, cap))
            rows = acc.shape[0]
            place = (iota((rows, W * cap), 0) + share * size).astype(F32)
            sel = jnp.where(ids == place, jnp.broadcast_to(scale, place.shape), 0.0).astype(BF16)
            q = buf[h, :, lo : lo + cap, :].astype(I32).astype(F32)
            if kind == 2:
                q = jnp.where(iota(q.shape, 1) < CAPW, q, 0.0)
            high, low = halves(q.reshape(W * cap, RANK))
            acc[...] += dot(sel, jnp.concatenate([high, low], axis=1).astype(BF16))

    pend.pop("ms")
    for g in GROUPS:
        for s in range(g * GROUP, (g + 1) * GROUP):
            if s > 0:
                ms_copy(s).wait_recv()
        ring_copy(0, g).start()
        sib_copy(0, g).start()

    pr_hop(3)
    pend.pop("fa")()
    out_f[...] = fall[...].reshape(FD, RANK)
    add_rows(mbuf, 0)
    for h in range(1, NY):
        for g in GROUPS:
            ring_copy(h - 1, g).wait_recv()
            if h < NY - 1:
                ring_copy(h, g).start()
            sib_copy(h, g).start()
        for g in range(groups):
            sib_copy(h - 1, g).wait_recv()
        add_rows(sbuf, h - 1)
        add_rows(mbuf, h)
    for g in range(groups):
        sib_copy(NY - 1, g).wait_recv()
    add_rows(sbuf, NY - 1)

    out_u[...] = 256.0 * accu[:, 0:RANK] + accu[:, RANK:] + gp[y]
    out_i[...] = 256.0 * acci[:, 0:RANK] + acci[:, RANK:]
    out_w[...] = 256.0 * accw[0:WS, 0:RANK] + accw[0:WS, RANK:]

    for h in range(NY - 1):
        for g in range(groups):
            ring_copy(h, g).wait_send()
    for h in range(NY):
        for g in range(groups):
            sib_copy(h, g).wait_send()
    for fn in pend.values():
        fn()
    for fn in leave:
        fn()


def finish(*refs):
    n = (len(refs) - 1) // 3
    src, dst, hold, sem = refs[:n], refs[n : 2 * n], refs[2 * n : 3 * n], refs[-1]
    inward = [pltpu.make_async_copy(src[k], hold[k], sem.at[0, k]) for k in range(n)]
    outward = [pltpu.make_async_copy(hold[k], dst[k], sem.at[1, k]) for k in range(n)]
    for cp in inward:
        cp.start()
    for k in range(n):
        inward[k].wait()
        outward[k].start()
    for cp in outward:
        cp.wait()


def local(
    W,
    NY,
    user_table,
    item_table,
    week_table,
    profile,
    feature_table,
    user_req,
    item_req,
    week_req,
    user_counts,
    item_counts,
    week_counts,
    pos_cells,
):
    UR, IR, WR = user_table.shape[0], item_table.shape[0], week_table.shape[0]
    FD = feature_table.shape[0]
    US, IS, WS = UR // (2 * NY), IR // (2 * NY), WR // (2 * NY)
    FC = FD // W
    groups = W // GROUP
    V, D = pltpu.VMEM, pltpu.SemaphoreType.DMA
    anywhere = pl.BlockSpec(memory_space=pl.ANY)
    vmem = pl.BlockSpec(memory_space=pltpu.VMEM)
    smem = pl.BlockSpec(memory_space=pltpu.SMEM)
    shapes = (
        jax.ShapeDtypeStruct((US, RANK), F32),
        jax.ShapeDtypeStruct((IS, RANK), F32),
        jax.ShapeDtypeStruct((WS, RANK), F32),
        jax.ShapeDtypeStruct((FD, RANK), F32),
    )
    outs = pl.pallas_call(
        functools.partial(kernel, W, NY),
        out_shape=shapes,
        in_specs=[anywhere] * 5 + [vmem] * 3 + [smem] * 3 + [vmem],
        out_specs=(vmem, vmem, vmem, vmem),
        scratch_shapes=[
            V((UR, RANK), BF16),
            V((IR, RANK), BF16),
            V((WR, RANK), BF16),
            V((UR, FD), BF16),
            V((FD, RANK), BF16),
            V((NY, US, FD), BF16),
            V((FD, RANK), BF16),
            V((W, 8, 128), I32),
            V((W, 8, 128), I32),
            V((W // 2 * CAPU, UR), BF16),
            V((W, MSG, RANK), BF16),
            V((W, MSG, RANK), BF16),
            V((NY, US, RANK), F32),
            V((NY - 1, US + 16, RANK), I16),
            V((NY - 1, US + 16, RANK), I16),
            V((RANK, FD), F32),
            V((W, FC, RANK), F32),
            V((W, FC, RANK), F32),
            V((W, FC, RANK), F32),
            V((32, 128), I32),
            V((32, 8, 128), I32),
            V((1, pos_cells.shape[1]), F32),
            V((32, 128, 128), I32),
            V((3 * BU, BI), F32),
            V((BU, BI), I32),
            V((BU, RANK), F32),
            V((32, RANK), F32),
            V((BI, RANK), BF16),
            V((RANK, BI), BF16),
            V((BU, RANK), F32),
            V((BI, RANK), F32),
            V((32, RANK), F32),
            V((PAIR * BU, RANK), BF16),
            V((PAIR * BU, RANK), BF16),
            V((PAIR * BU, BI), F32),
            V((PAIR * BU, BI), F32),
            V((PAIR * BU, BI), BF16),
            V((PAIR * BU, BI), BF16),
            V((W, MSG, RANK), I16),
            V((NY, W, MSG, RANK), I16),
            V((NY, W, MSG, RANK), I16),
            V((US, 2 * RANK), F32),
            V((IS, 2 * RANK), F32),
            V((16, 2 * RANK), F32),
            D((5,)),
            D((W,)),
            D((W,)),
            D((NY + 1,)),
            D((NY + 1,)),
            D((W,)),
            D((W,)),
            D((W,)),
            D((W,)),
            D((W,)),
            D((W,)),
            D((NY - 1,)),
            D((NY - 1,)),
            D((W,)),
            D((W,)),
            D((NY - 1, groups)),
            D((NY - 1, groups)),
            D((NY, groups)),
            D((NY, groups)),
        ],
        compiler_params=pltpu.CompilerParams(
            collective_id=0, has_side_effects=True, vmem_limit_bytes=56 << 20
        ),
    )(
        user_table,
        item_table,
        week_table,
        profile,
        feature_table,
        user_req[0],
        item_req[0],
        jnp.swapaxes(week_req[0], 0, 1),
        user_counts,
        item_counts,
        week_counts,
        pos_cells,
    )
    return pl.pallas_call(
        finish,
        out_shape=shapes,
        in_specs=[anywhere] * len(shapes),
        out_specs=(anywhere,) * len(shapes),
        scratch_shapes=[V(a.shape, a.dtype) for a in shapes] + [D((2, len(shapes)))],
    )(*outs)

def solution(mesh):
    W, NY = mesh.shape["wide"], mesh.shape["narrow"] // 2
    both = ("wide", "narrow")
    return jax.shard_map(
        functools.partial(local, W, NY),
        mesh=mesh,
        in_specs=(
            P("wide", None),
            P("wide", None),
            P("wide", None),
            P("wide", "narrow"),
            P("narrow", None),
            P(both, None, None),
            P(both, None, None),
            P(both, None, None),
            P(both, None),
            P(both, None),
            P(both, None),
            P(both, None),
        ),
        out_specs=(P(both, None), P(both, None), P(both, None), P("narrow", None)),
        check_vma=False,
    )
```

```python
import functools

import jax
import jax.numpy as jnp
from jax import lax
from jax.experimental import pallas as pl
from jax.experimental.pallas import tpu as pltpu
from jax.sharding import PartitionSpec as P

RANK = 256
BU = 256
BI = 256
BW = 28
CAPU = 32
CAPI = 32
CAPW = 4
CAPX = 16
MSG = CAPU + CAPI + CAPX
GROUP = 4
GROUPS = (0, 1, 3, 2)
FIELDS = 12
BLOCK = 4
THIRD = 3
PAIR = 2
SIDE = 4
ORDER = (1, 4, 3, 12, 5, 15, 7, 13, 2, 8, 9, 14, 11, 6, 10)
MESH = pl.DeviceIdType.MESH
F32, BF16, I32, I16 = jnp.float32, jnp.bfloat16, jnp.int32, jnp.int16


def dot(a, b):
    return jnp.dot(a, b, preferred_element_type=F32)


def dot_nt(a, b):
    return lax.dot_general(a, b, (((1,), (1,)), ((), ())), preferred_element_type=F32)


def dot_tn(a, b):
    return lax.dot_general(a, b, (((0,), (0,)), ((), ())), preferred_element_type=F32)


def iota(shape, axis):
    return lax.broadcasted_iota(I32, shape, axis)


def flat_index(counts, owners, place, cap):
    flat, end = place, 0
    for o in range(owners):
        c = counts[0, o]
        end = end + c
        flat = flat + jnp.where(place >= end, cap - c, 0)
    return flat


def halves(q):
    high = jnp.round(q * (1.0 / 256.0))
    return high, q - 256.0 * high


def exponent(top):
    return jnp.ceil(jnp.log2(jnp.maximum(top, 2.0**-100))) - 15.0


def quantize(x, e):
    return jnp.clip(jnp.round(x * jnp.exp2(-e)), -32767.0, 32767.0)


def kernel(
    W,
    NY,
    utab,
    itab,
    wtab,
    prof,
    ftab,
    ureq,
    ireq,
    wreq,
    ucnt,
    icnt,
    wcnt,
    pos,
    out_u,
    out_i,
    out_w,
    out_f,
    uv,
    iv,
    wv,
    xv,
    fv,
    x2,
    f2,
    reqs,
    rq,
    hot,
    rowsend,
    rowbuf,
    gp,
    pusend,
    puring,
    pisend,
    piring,
    feat,
    fsend,
    frecv,
    fall,
    pos_s,
    near,
    keep,
    spread,
    cacc,
    bits,
    uf,
    wf,
    vb,
    vt,
    gu,
    gv,
    gw,
    uw,
    gg,
    mm0,
    mm1,
    umsg,
    vmsg,
    umine,
    vmine,
    utheirs,
    vtheirs,
    uid,
    iid,
    wid,
    usc,
    isc,
    wsc,
    urh,
    irh,
    wrh,
    load_sem,
    req_ss,
    req_rs,
    x_ss,
    x_rs,
    row_ss,
    row_rs,
    fr_ss,
    fr_rs,
    fa_ss,
    fa_rs,
    pu_ss,
    pu_rs,
    pi_ss,
    pi_rs,
    mu_ss,
    mu_rs,
    mv_ss,
    mv_rs,
    su_ss,
    su_rs,
    sv_ss,
    sv_rs,
):
    me = lax.axis_index("wide")
    nar = lax.axis_index("narrow")
    y, c = nar // 2, nar % 2
    step = 1 - 2 * c
    nxt = lax.rem(y + step + NY, NY) * 2 + c
    prv = lax.rem(y - step + NY, NY) * 2 + c
    sib = y * 2 + 1 - c
    UR, IR, WR = uv.shape[0], iv.shape[0], wv.shape[0]
    FD = fv.shape[0]
    US, IS, WS = UR // (2 * NY), IR // (2 * NY), WR // (2 * NY)
    FC = FD // W

    X, Z = me // SIDE, lax.rem(me, SIDE)

    def to(s):
        return lax.rem(X + s // SIDE, SIDE) * SIDE + lax.rem(Z + s % SIDE, SIDE)

    def frm(s):
        return lax.rem(X + SIDE - s // SIDE, SIDE) * SIDE + lax.rem(Z + SIDE - s % SIDE, SIDE)

    def rcopy(src, dst, ss, rs, dev):
        return pltpu.make_async_remote_copy(
            src_ref=src,
            dst_ref=dst,
            send_sem=ss,
            recv_sem=rs,
            device_id=dev,
            device_id_type=MESH,
        )

    def peers(fn):
        for s in ORDER:
            fn(s)

    leave, pend = [], {}

    loads = [
        pltpu.make_async_copy(utab, uv, load_sem.at[0]),
        pltpu.make_async_copy(itab, iv, load_sem.at[1]),
        pltpu.make_async_copy(wtab, wv, load_sem.at[2]),
        pltpu.make_async_copy(ftab, fv, load_sem.at[3]),
        pltpu.make_async_copy(prof, xv, load_sem.at[4]),
    ]
    for cp in loads:
        cp.start()
    pend["tables"] = lambda: [cp.wait() for cp in loads[:3]]
    pend["profile"] = lambda: [cp.wait() for cp in loads[3:]]
    barrier = pltpu.get_barrier_semaphore()
    peers(
        lambda s: pl.semaphore_signal(
            barrier, inc=1, device_id={"wide": to(s)}, device_id_type=MESH
        )
    )
    for n in (nxt, prv, sib):
        pl.semaphore_signal(barrier, inc=1, device_id={"narrow": n}, device_id_type=MESH)
    for kind, ids in ((0, ureq[...]), (1, ireq[...])):
        line = jnp.concatenate([ids] * (128 // ids.shape[1]), axis=1)
        for o in range(W):
            reqs[o, kind : kind + 1, :] = line[o : o + 1, :]
    used = jnp.concatenate([wreq[...], jnp.zeros((CAPX - CAPW, W), I32)], axis=0)
    used = jnp.concatenate([used] * (128 // CAPX), axis=0)
    used = jnp.swapaxes(jnp.concatenate([used] * (128 // W), axis=1), 0, 1)
    for o in range(W):
        reqs[o, 2:3, :] = used[o : o + 1, :]
        reqs[o, 3:8, :] = jnp.zeros((5, 128), I32)
    pl.semaphore_wait(barrier, W - 1 + 3)

    def req_copy(s):
        return rcopy(
            reqs.at[to(s)],
            rq.at[s],
            req_ss.at[s],
            req_rs.at[s],
            {"wide": to(s)},
        )

    peers(lambda s: req_copy(s).start())
    rq[0] = reqs[me]
    leave.append(lambda: peers(lambda s: req_copy(s).wait_send()))
    pend["rq"] = lambda: peers(lambda s: req_copy(s).wait_recv())

    def x_copy(q):
        row = pl.multiple_of((2 * q + 1 - c) * US, US)
        return rcopy(
            prof.at[pl.ds(row, US), :], x2.at[q], x_ss.at[q], x_rs.at[q], {"narrow": sib}
        )

    f_copy = rcopy(ftab, f2, x_ss.at[NY], x_rs.at[NY], {"narrow": sib})
    f_copy.start()
    for q in range(NY):
        x_copy(q).start()

    def x_wait():
        f_copy.wait_recv()
        for q in range(NY):
            x_copy(q).wait_recv()

    def x_sent():
        f_copy.wait_send()
        for q in range(NY):
            x_copy(q).wait_send()

    pend["x"] = x_wait
    leave.append(x_sent)

    big = 1 << 30

    def least(xs):
        while len(xs) > 1:
            xs = [jnp.minimum(a, b) for a, b in zip(xs[::2], xs[1::2])]
        return xs[0]

    lines = pos.shape[1] // 128
    for k in range(lines):
        pos_s[k : k + 1, :] = pos[:, 128 * k : 128 * (k + 1)]
    near[...] = jnp.full(near.shape, big, I32)
    pt = jnp.swapaxes(
        jnp.concatenate([pos_s[...], jnp.zeros((128 - lines, 128), I32)], axis=0), 0, 1
    )
    for k in range(lines):
        spread[k] = jnp.broadcast_to(pt[:, k : k + 1], (128, 128))

    def compare(k, block, masked):
        for a in range(BLOCK):
            n = block * BLOCK + a
            row = jnp.broadcast_to(pos_s[pl.ds(n, 1), :], (8, 128))
            xs = []
            for t in range(16):
                x = spread[k, 8 * t : 8 * t + 8, :] ^ row
                if masked:
                    first = k * 128 + 8 * t + iota((8, 128), 0)
                    x = jnp.where(first < n * 128 + iota((8, 128), 1), x, big)
                xs.append(x)
            near[n] = jnp.minimum(near[n], least(xs))

    def column(k, z):
        own = k // BLOCK
        stop = jnp.minimum((own // THIRD + 1) * THIRD, lines // BLOCK)
        compare(k, own, True)
        lax.fori_loop(own + 1, stop, lambda b, y: (compare(k, b, False), y)[1], 0)
        return z

    lax.fori_loop(0, lines, column, 0)
    for k in range(lines):
        keep[:, 128 * k : 128 * (k + 1)] = jnp.min(near[k].astype(F32), axis=0, keepdims=True)
    pend.pop("tables")()
    pend.pop("rq")()
    RT = jnp.swapaxes(rq[...].reshape(W * 8, 128), 0, 1)

    def row_copy(s):
        return rcopy(
            rowsend.at[s],
            rowbuf.at[me],
            row_ss.at[s],
            row_rs.at[s],
            {"wide": frm(s)},
        )

    part = W // 2
    for m in range(2):
        slots = range(m * part, (m + 1) * part)
        for table, kind, cap, first in ((uv, 0, CAPU, 0), (iv, 1, CAPI, CAPU), (wv, 2, CAPX, CAPU + CAPI)):
            rows = table.shape[0]
            for a, s in enumerate(slots):
                col = jnp.broadcast_to(RT[0:cap, 8 * s + kind : 8 * s + kind + 1], (cap, rows))
                hot[a * cap : (a + 1) * cap, 0:rows] = jnp.where(
                    col == iota((cap, rows), 1), 1.0, 0.0
                ).astype(BF16)
            got = dot(hot[0 : part * cap, 0:rows], table[...]).astype(BF16)
            rowsend[m * part : (m + 1) * part, first : first + cap, :] = got.reshape(part, cap, RANK)
        for s in ORDER:
            if s in slots:
                row_copy(s).start()
    rowbuf[me] = rowsend[0]

    def row_wait(s):
        rcopy(
            rowsend.at[s],
            rowbuf.at[to(s)],
            row_ss.at[s],
            row_rs.at[s],
            {"wide": frm(s)},
        ).wait_recv()

    leave.append(lambda: peers(lambda s: row_copy(s).wait_send()))
    pend["row"] = lambda: peers(row_wait)

    pend.pop("profile")()
    feat[...] = jnp.zeros_like(feat)

    def resid(row, x, f):
        return (dot_nt(uv[pl.ds(row, US), :], f) - x.astype(F32)).astype(BF16)

    def own_rows(q, z):
        row = pl.multiple_of((2 * q + c) * US, US)
        r = resid(row, xv[pl.ds(row, US), :], fv[...])
        feat[...] += dot_tn(uv[pl.ds(row, US), :], r)
        gp[q] = 0.0625 * dot(r, fv[...])
        row = pl.multiple_of((2 * q + 1 - c) * US, US)
        r = resid(row, xv[pl.ds(row, US), :], fv[...])
        feat[...] += dot_tn(uv[pl.ds(row, US), :], r)
        return z

    lax.fori_loop(0, NY, own_rows, 0)
    fsend[...] = (0.0625 * jnp.swapaxes(feat[...], 0, 1)).reshape(W, FC, RANK)

    def fr_copy(s):
        return rcopy(
            fsend.at[to(s)],
            frecv.at[s],
            fr_ss.at[s],
            fr_rs.at[s],
            {"wide": to(s)},
        )

    peers(lambda s: fr_copy(s).start())
    frecv[0] = fsend[me]
    leave.append(lambda: peers(lambda s: fr_copy(s).wait_send()))
    pend["fr"] = lambda: peers(lambda s: fr_copy(s).wait_recv())
    pend.pop("x")()

    def sib_rows(q, z):
        row = pl.multiple_of((2 * q + c) * US, US)
        gp[q] += 0.0625 * dot(resid(row, x2[q], f2[...]), f2[...])
        return z

    lax.fori_loop(0, NY, sib_rows, 0)


    cacc[...] = jnp.zeros_like(cacc)

    def mark(n, z):
        at = pl.ds(pl.multiple_of(n * 512, 512), 512)
        p = pos[:, at]
        week, user, item = p >> 16, (p >> 8) & 255, p & 255
        part = week // FIELDS
        bit = jnp.left_shift(jnp.ones_like(week), 2 * (week - FIELDS * part))
        w = jnp.where(keep[:, at] > 0.5, bit.astype(F32), 0.0)
        row = iota((256, 512), 0)
        mine = jnp.where(row == user, 1.0, 0.0).astype(BF16)
        a = [mine * jnp.where(part == f, w, 0.0).astype(BF16) for f in range(3)]
        b = jnp.where(row == item, 1.0, 0.0).astype(BF16)
        cacc[...] += dot_nt(jnp.concatenate(a, axis=0), b)
        return z

    lax.fori_loop(0, pos.shape[1] // 512, mark, 0)

    def present(f):
        n = cacc[f * BU : (f + 1) * BU, :].astype(I32)
        return (n | (n >> 1)) & 0x555555

    bits[...] = present(0) | (present(1) << 1) | (present(2) << (2 * FIELDS))

    def pick(counts, n, cap):
        flat = flat_index(counts, W, iota((n, 1), 0), cap)
        return jnp.where(flat == iota((n, W * cap), 1), 1.0, 0.0).astype(BF16)

    pu, pv, pw = pick(ucnt, BU, CAPU), pick(icnt, BI, CAPI), pick(wcnt, 32, CAPX)

    pend.pop("row")()
    uf[...] = dot(pu, rowbuf[:, 0:CAPU, :].reshape(W * CAPU, RANK))
    vf = dot(pv, rowbuf[:, CAPU : CAPU + CAPI, :].reshape(W * CAPI, RANK))
    wf[...] = dot(pw, rowbuf[:, CAPU + CAPI : MSG, :].reshape(W * CAPX, RANK))
    vb[...] = (0.5 * vf).astype(BF16)
    vt[...] = (0.5 * jnp.swapaxes(vf, 0, 1)).astype(BF16)
    gu[...] = jnp.zeros_like(gu)
    gv[...] = jnp.zeros_like(gv)
    gw[...] = jnp.zeros_like(gw)

    def rows_of(k):
        return pl.ds(pl.multiple_of(k * BU, BU), PAIR * BU)

    def lead(k, mm):
        mixed = [(uf[...] * wf[pl.ds(k + a, 1), :]).astype(BF16) for a in range(PAIR)]
        mixed = jnp.concatenate(mixed, axis=0)
        uw[rows_of(k), :] = mixed
        mm[...] = dot(mixed, vt[...])

    def work(k, mm):
        place = jnp.where(
            k < FIELDS,
            2 * k,
            jnp.where(k < 2 * FIELDS, 2 * (k - FIELDS) + 1, 2 * (k - FIELDS)),
        )
        hits = bits[...] >> place
        parts = []
        for a in range(PAIR):
            sign = jnp.where((hits & (1 << (2 * a))) != 0, -1.0, 1.0)
            parts.append((jnp.tanh(mm[BU * a : BU * (a + 1), :]) + sign).astype(BF16))
        g = jnp.concatenate(parts, axis=0)
        gg[rows_of(k), :] = g
        q = dot(g, vb[...])
        total = gu[...]
        for a in range(PAIR):
            w, qa = wf[pl.ds(k + a, 1), :], q[BU * a : BU * (a + 1), :]
            total = total + qa * w
            gw[pl.ds(k + a, 1), :] = jnp.sum(qa * uf[...], axis=0, keepdims=True)
        gu[...] = total

    def weeks(lo, hi):
        def both(n, z):
            k = 2 * PAIR * n
            lead(k + PAIR, mm1)
            work(k, mm0)
            lead(k + 2 * PAIR, mm0)
            work(k + PAIR, mm1)
            return z

        lax.fori_loop(lo // (2 * PAIR), hi // (2 * PAIR), both, 0)

    lead(0, mm0)
    weeks(0, 12)

    pend.pop("fr")()
    total = frecv[0]
    for s in range(1, W):
        total = total + frecv[s]
    fall[me] = total

    def fa_copy(s):
        return rcopy(fall.at[me], fall.at[me], fa_ss.at[s], fa_rs.at[s], {"wide": to(s)})

    peers(lambda s: fa_copy(s).start())

    def fa_wait(s):
        rcopy(
            fall.at[me],
            fall.at[frm(s)],
            fa_ss.at[s],
            fa_rs.at[s],
            {"wide": to(s)},
        ).wait_recv()

    leave.append(lambda: peers(lambda s: fa_copy(s).wait_send()))
    pend["fa"] = lambda: peers(fa_wait)
    weeks(12, BW)

    def encode(g, counts, cap):
        n = g.shape[0]
        e = exponent(jnp.max(jnp.abs(g), axis=1, keepdims=True))
        high, low = halves(quantize(g, e))
        rhs = jnp.concatenate([high, low, jnp.broadcast_to(e, (n, 128))], axis=1).astype(BF16)
        flat = flat_index(counts, W, iota((1, n), 1), cap)
        sel = jnp.where(flat == iota((W * cap, n), 0), 1.0, 0.0).astype(BF16)
        got = dot(sel, rhs)
        code = (256.0 * got[:, 0:RANK] + got[:, RANK : 2 * RANK]).astype(I32)
        es = got[:, 2 * RANK :].reshape(W, cap, 128)
        es = jnp.where(iota((W, cap, 128), 1) == iota((W, cap, 128), 2) % cap, es, 0.0)
        es = jnp.sum(es, axis=1, keepdims=True).astype(I32)
        return code.reshape(W, cap, RANK), es

    def send_out(src, dst, ss, rs):
        def copy(t):
            return rcopy(src.at[to(t)], dst.at[t], ss.at[t], rs.at[t], {"wide": to(t)})

        peers(lambda t: copy(t).start())
        dst[0] = src[me]
        leave.append(lambda: peers(lambda t: copy(t).wait_send()))
        return copy

    ucode, ue = encode(gu[...], ucnt, CAPU)
    umsg[:, 0:CAPU, :] = ucode.astype(I16)
    wcode, we = encode(gw[...], wcnt, CAPX)
    shape = (W, CAPX, RANK)
    none = jnp.zeros_like(we)
    tail = wcode
    for r, left, right in (
        (8, reqs[:, 0:1, :], reqs[:, 1:2, :]),
        (9, reqs[:, 2:3, :], none),
        (10, ue, none),
        (11, we, none),
    ):
        line = jnp.broadcast_to(jnp.concatenate([left, right], axis=2), shape)
        tail = jnp.where(iota(shape, 1) == r, line, tail)
    umsg[:, CAPU:, :] = tail.astype(I16)
    mu_copy = send_out(umsg, umine, mu_ss, mu_rs)

    def value(n, z):
        at = pl.ds(pl.multiple_of(n * 4 * BU, BU), 4 * BU)
        gv[...] += dot_tn(gg[at, :], uw[at, :])
        return z

    lax.fori_loop(0, BW // 4, value, 0)
    vcode, ve = encode(0.5 * gv[...], icnt, CAPI)
    vmsg[:, 0:CAPI, :] = vcode.astype(I16)
    line = jnp.concatenate([ve, none], axis=2)
    vmsg[:, CAPI:, :] = jnp.broadcast_to(line, shape).astype(I16)
    mv_copy = send_out(vmsg, vmine, mv_ss, mv_rs)

    groups = W // GROUP

    def share_out(copy, mine, theirs, ss, rs):
        def sib_copy(g):
            at = pl.ds(g * GROUP, GROUP)
            return rcopy(mine.at[at], theirs.at[at], ss.at[g], rs.at[g], {"narrow": sib})

        for g in GROUPS:
            for t in range(g * GROUP, (g + 1) * GROUP):
                if t > 0:
                    copy(t).wait_recv()
            sib_copy(g).start()
            leave.append(lambda g=g: sib_copy(g).wait_send())
        return lambda: [sib_copy(g).wait_recv() for g in GROUPS]

    def lanes(tail_rows, r, first, cap):
        each = 128 // cap
        pieces = []
        for p in range(W // each):
            piece = jnp.zeros((1, 128), F32)
            for a in range(each):
                line = tail_rows[p * each + a, r : r + 1, first : first + 128]
                piece = jnp.where(iota((1, 128), 1) // cap == a, line, piece)
            pieces.append(piece)
        return jnp.concatenate(pieces, axis=1)

    def rows_in(buf, b, lo, cap, rhs):
        n = W * cap
        q = buf[:, lo : lo + cap, :].astype(I32).astype(F32)
        if lo > 0:
            q = jnp.where(iota(q.shape, 1) < CAPW, q, 0.0)
        high, low = halves(q.reshape(n, RANK))
        rhs[b * n : (b + 1) * n, 0:RANK] = high.astype(BF16)
        rhs[b * n : (b + 1) * n, RANK:] = low.astype(BF16)

    def unpack_u(buf, b):
        tail_rows = buf[:, CAPU:, :].astype(I32).astype(F32)
        nu, nw = slice(b * W * CAPU, (b + 1) * W * CAPU), slice(b * W * CAPX, (b + 1) * W * CAPX)
        uid[:, nu] = lanes(tail_rows, 8, 0, CAPU)
        iid[:, nu] = lanes(tail_rows, 8, 128, CAPI)
        wid[:, nw] = lanes(tail_rows, 9, 0, CAPX)
        usc[:, nu] = jnp.exp2(lanes(tail_rows, 10, 0, CAPU))
        wsc[:, nw] = jnp.exp2(lanes(tail_rows, 11, 0, CAPX))
        rows_in(buf, b, 0, CAPU, urh)
        rows_in(buf, b, CAPU, CAPX, wrh)

    def unpack_v(buf, b):
        tail_rows = buf[:, CAPI:, :].astype(I32).astype(F32)
        isc[:, b * W * CAPI : (b + 1) * W * CAPI] = jnp.exp2(lanes(tail_rows, 0, 0, CAPI))
        rows_in(buf, b, 0, CAPI, irh)

    def added(q, rows, size, ids, scale, rhs):
        row = iota((rows, ids.shape[1]), 0)
        place = row + (2 * q + c) * size
        if rows > size:
            place = jnp.where(row < size, place, -1)
        place = place.astype(F32)
        sel = jnp.where(ids[...] == place, jnp.broadcast_to(scale[...], place.shape), 0.0)
        both = dot(sel.astype(BF16), rhs[...])
        return 256.0 * both[:, 0:RANK] + both[:, RANK:]

    def pu_copy(h):
        return rcopy(pusend.at[h], puring.at[h], pu_ss.at[h], pu_rs.at[h], {"narrow": nxt})

    def pi_copy(h):
        return rcopy(pisend.at[h], piring.at[h], pi_ss.at[h], pi_rs.at[h], {"narrow": nxt})

    def coded(x):
        e = exponent(jnp.max(jnp.abs(x), axis=0, keepdims=True))
        line = jnp.broadcast_to(e, (16, RANK)).astype(I32).astype(I16)
        return quantize(x, e).astype(I32).astype(I16), line

    def plain(code, line):
        e = line.astype(I32).astype(F32)[0:1, :]
        return code.astype(I32).astype(F32) * jnp.exp2(e)

    def pu_start(h, x):
        pusend[h, 0:US, :], pusend[h, US:, :] = coded(x)
        pu_copy(h).start()
        leave.append(lambda: pu_copy(h).wait_send())

    def pi_start(h, x, w):
        pisend[h, 0:IS, :], pisend[h, IS : IS + 16, :] = coded(x)
        pisend[h, IS + 16 : IS + 32, :], pisend[h, IS + 32 :, :] = coded(w)
        pi_copy(h).start()
        leave.append(lambda: pi_copy(h).wait_send())

    def at_hop(h):
        return lax.rem(y - (h + 1) * step + 2 * NY, NY)

    def users(h):
        return added(at_hop(h), US, US, uid, usc, urh) + gp[at_hop(h)]

    def items(h):
        q = at_hop(h)
        return added(q, IS, IS, iid, isc, irh), added(q, 16, WS, wid, wsc, wrh)

    arrived = share_out(mu_copy, umine, utheirs, su_ss, su_rs)
    unpack_u(umine, 0)
    arrived()
    unpack_u(utheirs, 1)
    pu_start(0, users(0))
    arrived = share_out(mv_copy, vmine, vtheirs, sv_ss, sv_rs)
    unpack_v(vmine, 0)
    arrived()
    unpack_v(vtheirs, 1)
    pi_start(0, *items(0))
    pend.pop("fa")()
    out_f[...] = fall[...].reshape(FD, RANK)
    for h in range(1, NY):
        xu = users(h)
        pu_copy(h - 1).wait_recv()
        xu += plain(puring[h - 1, 0:US, :], puring[h - 1, US:, :])
        if h < NY - 1:
            pu_start(h, xu)
        else:
            out_u[...] = xu
        xi, xw = items(h)
        pi_copy(h - 1).wait_recv()
        xi += plain(piring[h - 1, 0:IS, :], piring[h - 1, IS : IS + 16, :])
        xw += plain(piring[h - 1, IS + 16 : IS + 32, :], piring[h - 1, IS + 32 :, :])
        if h < NY - 1:
            pi_start(h, xi, xw)
        else:
            out_i[...] = xi
            out_w[...] = xw[0:WS, :]

    for fn in pend.values():
        fn()
    for fn in leave:
        fn()


def finish(*refs):
    n = (len(refs) - 1) // 3
    src, dst, hold, sem = refs[:n], refs[n : 2 * n], refs[2 * n : 3 * n], refs[-1]
    inward = [pltpu.make_async_copy(src[k], hold[k], sem.at[0, k]) for k in range(n)]
    outward = [pltpu.make_async_copy(hold[k], dst[k], sem.at[1, k]) for k in range(n)]
    for cp in inward:
        cp.start()
    for k in range(n):
        inward[k].wait()
        outward[k].start()
    for cp in outward:
        cp.wait()


def local(
    W,
    NY,
    user_table,
    item_table,
    week_table,
    profile,
    feature_table,
    user_req,
    item_req,
    week_req,
    user_counts,
    item_counts,
    week_counts,
    pos_cells,
):
    UR, IR, WR = user_table.shape[0], item_table.shape[0], week_table.shape[0]
    FD = feature_table.shape[0]
    US, IS, WS = UR // (2 * NY), IR // (2 * NY), WR // (2 * NY)
    FC = FD // W
    groups = W // GROUP
    V, D = pltpu.VMEM, pltpu.SemaphoreType.DMA
    anywhere = pl.BlockSpec(memory_space=pl.ANY)
    vmem = pl.BlockSpec(memory_space=pltpu.VMEM)
    smem = pl.BlockSpec(memory_space=pltpu.SMEM)
    shapes = (
        jax.ShapeDtypeStruct((US, RANK), F32),
        jax.ShapeDtypeStruct((IS, RANK), F32),
        jax.ShapeDtypeStruct((WS, RANK), F32),
        jax.ShapeDtypeStruct((FD, RANK), F32),
    )
    outs = pl.pallas_call(
        functools.partial(kernel, W, NY),
        out_shape=shapes,
        in_specs=[anywhere] * 5 + [vmem] * 3 + [smem] * 3 + [vmem],
        out_specs=(vmem, vmem, vmem, vmem),
        scratch_shapes=[
            V((UR, RANK), BF16),
            V((IR, RANK), BF16),
            V((WR, RANK), BF16),
            V((UR, FD), BF16),
            V((FD, RANK), BF16),
            V((NY, US, FD), BF16),
            V((FD, RANK), BF16),
            V((W, 8, 128), I32),
            V((W, 8, 128), I32),
            V((W // 2 * CAPU, UR), BF16),
            V((W, MSG, RANK), BF16),
            V((W, MSG, RANK), BF16),
            V((NY, US, RANK), F32),
            V((NY - 1, US + 16, RANK), I16),
            V((NY - 1, US + 16, RANK), I16),
            V((NY - 1, IS + 48, RANK), I16),
            V((NY - 1, IS + 48, RANK), I16),
            V((RANK, FD), F32),
            V((W, FC, RANK), F32),
            V((W, FC, RANK), F32),
            V((W, FC, RANK), F32),
            V((32, 128), I32),
            V((32, 8, 128), I32),
            V((1, pos_cells.shape[1]), F32),
            V((32, 128, 128), I32),
            V((3 * BU, BI), F32),
            V((BU, BI), I32),
            V((BU, RANK), F32),
            V((32, RANK), F32),
            V((BI, RANK), BF16),
            V((RANK, BI), BF16),
            V((BU, RANK), F32),
            V((BI, RANK), F32),
            V((32, RANK), F32),
            V(((BW + PAIR) * BU, RANK), BF16),
            V((BW * BU, BI), BF16),
            V((PAIR * BU, BI), F32),
            V((PAIR * BU, BI), F32),
            V((W, CAPU + CAPX, RANK), I16),
            V((W, CAPI + CAPX, RANK), I16),
            V((W, CAPU + CAPX, RANK), I16),
            V((W, CAPI + CAPX, RANK), I16),
            V((W, CAPU + CAPX, RANK), I16),
            V((W, CAPI + CAPX, RANK), I16),
            V((1, 2 * W * CAPU), F32),
            V((1, 2 * W * CAPI), F32),
            V((1, 2 * W * CAPX), F32),
            V((1, 2 * W * CAPU), F32),
            V((1, 2 * W * CAPI), F32),
            V((1, 2 * W * CAPX), F32),
            V((2 * W * CAPU, 2 * RANK), BF16),
            V((2 * W * CAPI, 2 * RANK), BF16),
            V((2 * W * CAPX, 2 * RANK), BF16),
            D((5,)),
            D((W,)),
            D((W,)),
            D((NY + 1,)),
            D((NY + 1,)),
            D((W,)),
            D((W,)),
            D((W,)),
            D((W,)),
            D((W,)),
            D((W,)),
            D((NY - 1,)),
            D((NY - 1,)),
            D((NY - 1,)),
            D((NY - 1,)),
            D((W,)),
            D((W,)),
            D((W,)),
            D((W,)),
            D((groups,)),
            D((groups,)),
            D((groups,)),
            D((groups,)),
        ],
        compiler_params=pltpu.CompilerParams(
            collective_id=0, has_side_effects=True, vmem_limit_bytes=56 << 20
        ),
    )(
        user_table,
        item_table,
        week_table,
        profile,
        feature_table,
        user_req[0],
        item_req[0],
        jnp.swapaxes(week_req[0], 0, 1),
        user_counts,
        item_counts,
        week_counts,
        pos_cells,
    )
    return pl.pallas_call(
        finish,
        out_shape=shapes,
        in_specs=[anywhere] * len(shapes),
        out_specs=(anywhere,) * len(shapes),
        scratch_shapes=[V(a.shape, a.dtype) for a in shapes] + [D((2, len(shapes)))],
    )(*outs)

def solution(mesh):
    W, NY = mesh.shape["wide"], mesh.shape["narrow"] // 2
    both = ("wide", "narrow")
    return jax.shard_map(
        functools.partial(local, W, NY),
        mesh=mesh,
        in_specs=(
            P("wide", None),
            P("wide", None),
            P("wide", None),
            P("wide", "narrow"),
            P("narrow", None),
            P(both, None, None),
            P(both, None, None),
            P(both, None, None),
            P(both, None),
            P(both, None),
            P(both, None),
            P(both, None),
        ),
        out_specs=(P(both, None), P(both, None), P(both, None), P("narrow", None)),
        check_vma=False,
    )
```

```python
import functools

import jax
import jax.numpy as jnp
from jax import lax
from jax.experimental import pallas as pl
from jax.experimental.pallas import tpu as pltpu
from jax.sharding import PartitionSpec as P

RANK = 256
BU = 256
BI = 256
BW = 28
CAPU = 32
CAPI = 32
CAPW = 4
CAPX = 16
MSG = CAPU + CAPI + CAPX
GROUP = 4
GROUPS = (0, 1, 3, 2)
FIELDS = 12
BLOCK = 4
THIRD = 3
PAIR = 2
SIDE = 4
ORDER = (1, 4, 3, 12, 5, 15, 7, 13, 2, 8, 9, 14, 11, 6, 10)
MESH = pl.DeviceIdType.MESH
F32, BF16, I32, I16 = jnp.float32, jnp.bfloat16, jnp.int32, jnp.int16


def dot(a, b):
    return jnp.dot(a, b, preferred_element_type=F32)


def dot_nt(a, b):
    return lax.dot_general(a, b, (((1,), (1,)), ((), ())), preferred_element_type=F32)


def dot_tn(a, b):
    return lax.dot_general(a, b, (((0,), (0,)), ((), ())), preferred_element_type=F32)


def iota(shape, axis):
    return lax.broadcasted_iota(I32, shape, axis)


def flat_index(counts, owners, place, cap):
    flat, end = place, 0
    for o in range(owners):
        c = counts[0, o]
        end = end + c
        flat = flat + jnp.where(place >= end, cap - c, 0)
    return flat


def halves(q):
    high = jnp.round(q * (1.0 / 256.0))
    return high, q - 256.0 * high


def exponent(top):
    return jnp.ceil(jnp.log2(jnp.maximum(top, 2.0**-100))) - 15.0


def quantize(x, e):
    return jnp.clip(jnp.round(x * jnp.exp2(-e)), -32767.0, 32767.0)


def kernel(
    W,
    NY,
    utab,
    itab,
    wtab,
    prof,
    ftab,
    ureq,
    ireq,
    wreq,
    ucnt,
    icnt,
    wcnt,
    pos,
    out_u,
    out_i,
    out_w,
    out_f,
    uv,
    iv,
    wv,
    xv,
    fv,
    x2,
    f2,
    reqs,
    rq,
    hot,
    rowsend,
    rowbuf,
    gp,
    pusend,
    puring,
    pisend,
    piring,
    feat,
    fsend,
    frecv,
    fall,
    pos_s,
    near,
    keep,
    spread,
    cacc,
    bits,
    uf,
    wf,
    vb,
    vt,
    gu,
    gv,
    gw,
    uw,
    gg,
    mm0,
    mm1,
    umsg,
    vmsg,
    umine,
    vmine,
    utheirs,
    vtheirs,
    uid,
    iid,
    wid,
    usc,
    isc,
    wsc,
    urh,
    irh,
    wrh,
    load_sem,
    req_ss,
    req_rs,
    x_ss,
    x_rs,
    row_ss,
    row_rs,
    fr_ss,
    fr_rs,
    fa_ss,
    fa_rs,
    pu_ss,
    pu_rs,
    pi_ss,
    pi_rs,
    mu_ss,
    mu_rs,
    mv_ss,
    mv_rs,
    su_ss,
    su_rs,
    sv_ss,
    sv_rs,
):
    me = lax.axis_index("wide")
    nar = lax.axis_index("narrow")
    y, c = nar // 2, nar % 2
    step = 1 - 2 * c
    nxt = lax.rem(y + step + NY, NY) * 2 + c
    prv = lax.rem(y - step + NY, NY) * 2 + c
    sib = y * 2 + 1 - c
    UR, IR, WR = uv.shape[0], iv.shape[0], wv.shape[0]
    FD = fv.shape[0]
    US, IS, WS = UR // (2 * NY), IR // (2 * NY), WR // (2 * NY)
    FC = FD // W

    X, Z = me // SIDE, lax.rem(me, SIDE)

    def to(s):
        return lax.rem(X + s // SIDE, SIDE) * SIDE + lax.rem(Z + s % SIDE, SIDE)

    def frm(s):
        return lax.rem(X + SIDE - s // SIDE, SIDE) * SIDE + lax.rem(Z + SIDE - s % SIDE, SIDE)

    def rcopy(src, dst, ss, rs, dev):
        return pltpu.make_async_remote_copy(
            src_ref=src,
            dst_ref=dst,
            send_sem=ss,
            recv_sem=rs,
            device_id=dev,
            device_id_type=MESH,
        )

    def peers(fn):
        for s in ORDER:
            fn(s)

    leave, pend = [], {}

    loads = [
        pltpu.make_async_copy(utab, uv, load_sem.at[0]),
        pltpu.make_async_copy(itab, iv, load_sem.at[1]),
        pltpu.make_async_copy(wtab, wv, load_sem.at[2]),
        pltpu.make_async_copy(ftab, fv, load_sem.at[3]),
        pltpu.make_async_copy(prof, xv, load_sem.at[4]),
    ]
    for cp in loads:
        cp.start()
    pend["tables"] = lambda: [cp.wait() for cp in loads[:3]]
    pend["profile"] = lambda: [cp.wait() for cp in loads[3:]]
    barrier = pltpu.get_barrier_semaphore()
    peers(
        lambda s: pl.semaphore_signal(
            barrier, inc=1, device_id={"wide": to(s)}, device_id_type=MESH
        )
    )
    for n in (nxt, prv, sib):
        pl.semaphore_signal(barrier, inc=1, device_id={"narrow": n}, device_id_type=MESH)
    for kind, ids in ((0, ureq[...]), (1, ireq[...])):
        line = jnp.concatenate([ids] * (128 // ids.shape[1]), axis=1)
        for o in range(W):
            reqs[o, kind : kind + 1, :] = line[o : o + 1, :]
    used = jnp.concatenate([wreq[...], jnp.zeros((CAPX - CAPW, W), I32)], axis=0)
    used = jnp.concatenate([used] * (128 // CAPX), axis=0)
    used = jnp.swapaxes(jnp.concatenate([used] * (128 // W), axis=1), 0, 1)
    for o in range(W):
        reqs[o, 2:3, :] = used[o : o + 1, :]
        reqs[o, 3:8, :] = jnp.zeros((5, 128), I32)
    pl.semaphore_wait(barrier, W - 1 + 3)

    def req_copy(s):
        return rcopy(
            reqs.at[to(s)],
            rq.at[s],
            req_ss.at[s],
            req_rs.at[s],
            {"wide": to(s)},
        )

    peers(lambda s: req_copy(s).start())
    rq[0] = reqs[me]
    leave.append(lambda: peers(lambda s: req_copy(s).wait_send()))
    pend["rq"] = lambda: peers(lambda s: req_copy(s).wait_recv())

    def x_copy(q):
        row = pl.multiple_of((2 * q + 1 - c) * US, US)
        return rcopy(
            prof.at[pl.ds(row, US), :], x2.at[q], x_ss.at[q], x_rs.at[q], {"narrow": sib}
        )

    f_copy = rcopy(ftab, f2, x_ss.at[NY], x_rs.at[NY], {"narrow": sib})
    f_copy.start()
    for q in range(NY):
        x_copy(q).start()

    def x_wait():
        f_copy.wait_recv()
        for q in range(NY):
            x_copy(q).wait_recv()

    def x_sent():
        f_copy.wait_send()
        for q in range(NY):
            x_copy(q).wait_send()

    pend["x"] = x_wait
    leave.append(x_sent)

    big = 1 << 30

    def least(xs):
        while len(xs) > 1:
            xs = [jnp.minimum(a, b) for a, b in zip(xs[::2], xs[1::2])]
        return xs[0]

    lines = pos.shape[1] // 128
    for k in range(lines):
        pos_s[k : k + 1, :] = pos[:, 128 * k : 128 * (k + 1)]
    near[...] = jnp.full(near.shape, big, I32)
    pt = jnp.swapaxes(
        jnp.concatenate([pos_s[...], jnp.zeros((128 - lines, 128), I32)], axis=0), 0, 1
    )
    for k in range(lines):
        spread[k] = jnp.broadcast_to(pt[:, k : k + 1], (128, 128))

    def compare(k, block, masked):
        for a in range(BLOCK):
            n = block * BLOCK + a
            row = jnp.broadcast_to(pos_s[pl.ds(n, 1), :], (8, 128))
            xs = []
            for t in range(16):
                x = spread[k, 8 * t : 8 * t + 8, :] ^ row
                if masked:
                    first = k * 128 + 8 * t + iota((8, 128), 0)
                    x = jnp.where(first < n * 128 + iota((8, 128), 1), x, big)
                xs.append(x)
            near[n] = jnp.minimum(near[n], least(xs))

    def column(k, z):
        own = k // BLOCK
        stop = jnp.minimum((own // THIRD + 1) * THIRD, lines // BLOCK)
        compare(k, own, True)
        lax.fori_loop(own + 1, stop, lambda b, y: (compare(k, b, False), y)[1], 0)
        return z

    lax.fori_loop(0, lines, column, 0)
    for k in range(lines):
        keep[:, 128 * k : 128 * (k + 1)] = jnp.min(near[k].astype(F32), axis=0, keepdims=True)
    pend.pop("tables")()
    pend.pop("rq")()
    RT = jnp.swapaxes(rq[...].reshape(W * 8, 128), 0, 1)

    def row_copy(s):
        return rcopy(
            rowsend.at[s],
            rowbuf.at[me],
            row_ss.at[s],
            row_rs.at[s],
            {"wide": frm(s)},
        )

    part = W // 2
    for m in range(2):
        slots = range(m * part, (m + 1) * part)
        for table, kind, cap, first in ((uv, 0, CAPU, 0), (iv, 1, CAPI, CAPU), (wv, 2, CAPX, CAPU + CAPI)):
            rows = table.shape[0]
            for a, s in enumerate(slots):
                col = jnp.broadcast_to(RT[0:cap, 8 * s + kind : 8 * s + kind + 1], (cap, rows))
                hot[a * cap : (a + 1) * cap, 0:rows] = jnp.where(
                    col == iota((cap, rows), 1), 1.0, 0.0
                ).astype(BF16)
            got = dot(hot[0 : part * cap, 0:rows], table[...]).astype(BF16)
            rowsend[m * part : (m + 1) * part, first : first + cap, :] = got.reshape(part, cap, RANK)
        for s in ORDER:
            if s in slots:
                row_copy(s).start()
    rowbuf[me] = rowsend[0]

    def row_wait(s):
        rcopy(
            rowsend.at[s],
            rowbuf.at[to(s)],
            row_ss.at[s],
            row_rs.at[s],
            {"wide": frm(s)},
        ).wait_recv()

    leave.append(lambda: peers(lambda s: row_copy(s).wait_send()))
    pend["row"] = lambda: peers(row_wait)

    pend.pop("profile")()
    feat[...] = jnp.zeros_like(feat)

    def resid(row, x, f):
        return (dot_nt(uv[pl.ds(row, US), :], f) - x.astype(F32)).astype(BF16)

    def own_rows(q, z):
        row = pl.multiple_of((2 * q + c) * US, US)
        r = resid(row, xv[pl.ds(row, US), :], fv[...])
        feat[...] += dot_tn(uv[pl.ds(row, US), :], r)
        gp[q] = 0.0625 * dot(r, fv[...])
        row = pl.multiple_of((2 * q + 1 - c) * US, US)
        r = resid(row, xv[pl.ds(row, US), :], fv[...])
        feat[...] += dot_tn(uv[pl.ds(row, US), :], r)
        return z

    lax.fori_loop(0, NY, own_rows, 0)
    fsend[...] = (0.0625 * jnp.swapaxes(feat[...], 0, 1)).reshape(W, FC, RANK)

    def fr_copy(s):
        return rcopy(
            fsend.at[to(s)],
            frecv.at[s],
            fr_ss.at[s],
            fr_rs.at[s],
            {"wide": to(s)},
        )


    cacc[...] = jnp.zeros_like(cacc)

    def mark(n, z):
        at = pl.ds(pl.multiple_of(n * 512, 512), 512)
        p = pos[:, at]
        week, user, item = p >> 16, (p >> 8) & 255, p & 255
        part = week // FIELDS
        bit = jnp.left_shift(jnp.ones_like(week), 2 * (week - FIELDS * part))
        w = jnp.where(keep[:, at] > 0.5, bit.astype(F32), 0.0)
        row = iota((256, 512), 0)
        mine = jnp.where(row == user, 1.0, 0.0).astype(BF16)
        a = [mine * jnp.where(part == f, w, 0.0).astype(BF16) for f in range(3)]
        b = jnp.where(row == item, 1.0, 0.0).astype(BF16)
        cacc[...] += dot_nt(jnp.concatenate(a, axis=0), b)
        return z

    lax.fori_loop(0, pos.shape[1] // 512, mark, 0)

    def present(f):
        n = cacc[f * BU : (f + 1) * BU, :].astype(I32)
        return (n | (n >> 1)) & 0x555555

    bits[...] = present(0) | (present(1) << 1) | (present(2) << (2 * FIELDS))

    def pick(counts, n, cap):
        flat = flat_index(counts, W, iota((n, 1), 0), cap)
        return jnp.where(flat == iota((n, W * cap), 1), 1.0, 0.0).astype(BF16)

    pu, pv, pw = pick(ucnt, BU, CAPU), pick(icnt, BI, CAPI), pick(wcnt, 32, CAPX)

    pend.pop("row")()
    peers(lambda s: fr_copy(s).start())
    frecv[0] = fsend[me]
    leave.append(lambda: peers(lambda s: fr_copy(s).wait_send()))
    pend["fr"] = lambda: peers(lambda s: fr_copy(s).wait_recv())
    uf[...] = dot(pu, rowbuf[:, 0:CAPU, :].reshape(W * CAPU, RANK))
    vf = dot(pv, rowbuf[:, CAPU : CAPU + CAPI, :].reshape(W * CAPI, RANK))
    wf[...] = dot(pw, rowbuf[:, CAPU + CAPI : MSG, :].reshape(W * CAPX, RANK))
    vb[...] = (0.5 * vf).astype(BF16)
    vt[...] = (0.5 * jnp.swapaxes(vf, 0, 1)).astype(BF16)
    gu[...] = jnp.zeros_like(gu)
    gv[...] = jnp.zeros_like(gv)
    gw[...] = jnp.zeros_like(gw)

    def rows_of(k):
        return pl.ds(pl.multiple_of(k * BU, BU), PAIR * BU)

    def lead(k, mm):
        mixed = [(uf[...] * wf[pl.ds(k + a, 1), :]).astype(BF16) for a in range(PAIR)]
        mixed = jnp.concatenate(mixed, axis=0)
        uw[rows_of(k), :] = mixed
        mm[...] = dot(mixed, vt[...])

    def work(k, mm):
        place = jnp.where(
            k < FIELDS,
            2 * k,
            jnp.where(k < 2 * FIELDS, 2 * (k - FIELDS) + 1, 2 * (k - FIELDS)),
        )
        hits = bits[...] >> place
        parts = []
        for a in range(PAIR):
            sign = jnp.where((hits & (1 << (2 * a))) != 0, -1.0, 1.0)
            parts.append((jnp.tanh(mm[BU * a : BU * (a + 1), :]) + sign).astype(BF16))
        g = jnp.concatenate(parts, axis=0)
        gg[rows_of(k), :] = g
        q = dot(g, vb[...])
        total = gu[...]
        for a in range(PAIR):
            w, qa = wf[pl.ds(k + a, 1), :], q[BU * a : BU * (a + 1), :]
            total = total + qa * w
            gw[pl.ds(k + a, 1), :] = jnp.sum(qa * uf[...], axis=0, keepdims=True)
        gu[...] = total

    def weeks(lo, hi):
        def both(n, z):
            k = 2 * PAIR * n
            lead(k + PAIR, mm1)
            work(k, mm0)
            lead(k + 2 * PAIR, mm0)
            work(k + PAIR, mm1)
            return z

        lax.fori_loop(lo // (2 * PAIR), hi // (2 * PAIR), both, 0)

    lead(0, mm0)
    weeks(0, BW)

    def encode(g, counts, cap):
        n = g.shape[0]
        e = exponent(jnp.max(jnp.abs(g), axis=1, keepdims=True))
        high, low = halves(quantize(g, e))
        rhs = jnp.concatenate([high, low, jnp.broadcast_to(e, (n, 128))], axis=1).astype(BF16)
        flat = flat_index(counts, W, iota((1, n), 1), cap)
        sel = jnp.where(flat == iota((W * cap, n), 0), 1.0, 0.0).astype(BF16)
        got = dot(sel, rhs)
        code = (256.0 * got[:, 0:RANK] + got[:, RANK : 2 * RANK]).astype(I32)
        es = got[:, 2 * RANK :].reshape(W, cap, 128)
        es = jnp.where(iota((W, cap, 128), 1) == iota((W, cap, 128), 2) % cap, es, 0.0)
        es = jnp.sum(es, axis=1, keepdims=True).astype(I32)
        return code.reshape(W, cap, RANK), es

    def send_out(src, dst, ss, rs):
        def copy(t):
            return rcopy(src.at[to(t)], dst.at[t], ss.at[t], rs.at[t], {"wide": to(t)})

        peers(lambda t: copy(t).start())
        dst[0] = src[me]
        leave.append(lambda: peers(lambda t: copy(t).wait_send()))
        return copy

    ucode, ue = encode(gu[...], ucnt, CAPU)
    umsg[:, 0:CAPU, :] = ucode.astype(I16)
    wcode, we = encode(gw[...], wcnt, CAPX)
    shape = (W, CAPX, RANK)
    none = jnp.zeros_like(we)
    tail = wcode
    for r, left, right in (
        (8, reqs[:, 0:1, :], reqs[:, 1:2, :]),
        (9, reqs[:, 2:3, :], none),
        (10, ue, none),
        (11, we, none),
    ):
        line = jnp.broadcast_to(jnp.concatenate([left, right], axis=2), shape)
        tail = jnp.where(iota(shape, 1) == r, line, tail)
    umsg[:, CAPU:, :] = tail.astype(I16)
    mu_copy = send_out(umsg, umine, mu_ss, mu_rs)

    def value(n, z):
        at = pl.ds(pl.multiple_of(n * 4 * BU, BU), 4 * BU)
        gv[...] += dot_tn(gg[at, :], uw[at, :])
        return z

    lax.fori_loop(0, BW // 4, value, 0)
    vcode, ve = encode(0.5 * gv[...], icnt, CAPI)
    vmsg[:, 0:CAPI, :] = vcode.astype(I16)
    line = jnp.concatenate([ve, none], axis=2)
    vmsg[:, CAPI:, :] = jnp.broadcast_to(line, shape).astype(I16)
    mv_copy = send_out(vmsg, vmine, mv_ss, mv_rs)

    pend.pop("x")()

    def sib_rows(q, z):
        row = pl.multiple_of((2 * q + c) * US, US)
        gp[q] += 0.0625 * dot(resid(row, x2[q], f2[...]), f2[...])
        return z

    lax.fori_loop(0, NY, sib_rows, 0)


    pend.pop("fr")()
    total = frecv[0]
    for s in range(1, W):
        total = total + frecv[s]
    fall[me] = total

    def fa_copy(s):
        return rcopy(fall.at[me], fall.at[me], fa_ss.at[s], fa_rs.at[s], {"wide": to(s)})

    peers(lambda s: fa_copy(s).start())

    def fa_wait(s):
        rcopy(
            fall.at[me],
            fall.at[frm(s)],
            fa_ss.at[s],
            fa_rs.at[s],
            {"wide": to(s)},
        ).wait_recv()

    leave.append(lambda: peers(lambda s: fa_copy(s).wait_send()))
    pend["fa"] = lambda: peers(fa_wait)

    groups = W // GROUP

    def share_out(copy, mine, theirs, ss, rs):
        def sib_copy(g):
            at = pl.ds(g * GROUP, GROUP)
            return rcopy(mine.at[at], theirs.at[at], ss.at[g], rs.at[g], {"narrow": sib})

        for g in GROUPS:
            for t in range(g * GROUP, (g + 1) * GROUP):
                if t > 0:
                    copy(t).wait_recv()
            sib_copy(g).start()
            leave.append(lambda g=g: sib_copy(g).wait_send())
        return lambda: [sib_copy(g).wait_recv() for g in GROUPS]

    def lanes(tail_rows, r, first, cap):
        each = 128 // cap
        pieces = []
        for p in range(W // each):
            piece = jnp.zeros((1, 128), F32)
            for a in range(each):
                line = tail_rows[p * each + a, r : r + 1, first : first + 128]
                piece = jnp.where(iota((1, 128), 1) // cap == a, line, piece)
            pieces.append(piece)
        return jnp.concatenate(pieces, axis=1)

    def rows_in(buf, b, lo, cap, rhs):
        n = W * cap
        q = buf[:, lo : lo + cap, :].astype(I32).astype(F32)
        if lo > 0:
            q = jnp.where(iota(q.shape, 1) < CAPW, q, 0.0)
        high, low = halves(q.reshape(n, RANK))
        rhs[b * n : (b + 1) * n, 0:RANK] = high.astype(BF16)
        rhs[b * n : (b + 1) * n, RANK:] = low.astype(BF16)

    def unpack_u(buf, b):
        tail_rows = buf[:, CAPU:, :].astype(I32).astype(F32)
        nu, nw = slice(b * W * CAPU, (b + 1) * W * CAPU), slice(b * W * CAPX, (b + 1) * W * CAPX)
        uid[:, nu] = lanes(tail_rows, 8, 0, CAPU)
        iid[:, nu] = lanes(tail_rows, 8, 128, CAPI)
        wid[:, nw] = lanes(tail_rows, 9, 0, CAPX)
        usc[:, nu] = jnp.exp2(lanes(tail_rows, 10, 0, CAPU))
        wsc[:, nw] = jnp.exp2(lanes(tail_rows, 11, 0, CAPX))
        rows_in(buf, b, 0, CAPU, urh)
        rows_in(buf, b, CAPU, CAPX, wrh)

    def unpack_v(buf, b):
        tail_rows = buf[:, CAPI:, :].astype(I32).astype(F32)
        isc[:, b * W * CAPI : (b + 1) * W * CAPI] = jnp.exp2(lanes(tail_rows, 0, 0, CAPI))
        rows_in(buf, b, 0, CAPI, irh)

    def added(q, rows, size, ids, scale, rhs):
        row = iota((rows, ids.shape[1]), 0)
        place = row + (2 * q + c) * size
        if rows > size:
            place = jnp.where(row < size, place, -1)
        place = place.astype(F32)
        sel = jnp.where(ids[...] == place, jnp.broadcast_to(scale[...], place.shape), 0.0)
        both = dot(sel.astype(BF16), rhs[...])
        return 256.0 * both[:, 0:RANK] + both[:, RANK:]

    def pu_copy(h):
        return rcopy(pusend.at[h], puring.at[h], pu_ss.at[h], pu_rs.at[h], {"narrow": nxt})

    def pi_copy(h):
        return rcopy(pisend.at[h], piring.at[h], pi_ss.at[h], pi_rs.at[h], {"narrow": nxt})

    def coded(x):
        e = exponent(jnp.max(jnp.abs(x), axis=0, keepdims=True))
        line = jnp.broadcast_to(e, (16, RANK)).astype(I32).astype(I16)
        return quantize(x, e).astype(I32).astype(I16), line

    def plain(code, line):
        e = line.astype(I32).astype(F32)[0:1, :]
        return code.astype(I32).astype(F32) * jnp.exp2(e)

    def pu_start(h, x):
        pusend[h, 0:US, :], pusend[h, US:, :] = coded(x)
        pu_copy(h).start()
        leave.append(lambda: pu_copy(h).wait_send())

    def pi_start(h, x, w):
        pisend[h, 0:IS, :], pisend[h, IS : IS + 16, :] = coded(x)
        pisend[h, IS + 16 : IS + 32, :], pisend[h, IS + 32 :, :] = coded(w)
        pi_copy(h).start()
        leave.append(lambda: pi_copy(h).wait_send())

    def at_hop(h):
        return lax.rem(y - (h + 1) * step + 2 * NY, NY)

    def users(h):
        return added(at_hop(h), US, US, uid, usc, urh) + gp[at_hop(h)]

    def items(h):
        q = at_hop(h)
        return added(q, IS, IS, iid, isc, irh), added(q, 16, WS, wid, wsc, wrh)

    arrived = share_out(mu_copy, umine, utheirs, su_ss, su_rs)
    unpack_u(umine, 0)
    arrived()
    unpack_u(utheirs, 1)
    pu_start(0, users(0))
    arrived = share_out(mv_copy, vmine, vtheirs, sv_ss, sv_rs)
    unpack_v(vmine, 0)
    arrived()
    unpack_v(vtheirs, 1)
    pi_start(0, *items(0))
    for h in range(1, NY):
        xu = users(h)
        if h == NY - 1:
            pend.pop("fa")()
            out_f[...] = fall[...].reshape(FD, RANK)
        pu_copy(h - 1).wait_recv()
        xu += plain(puring[h - 1, 0:US, :], puring[h - 1, US:, :])
        if h < NY - 1:
            pu_start(h, xu)
        else:
            out_u[...] = xu
        xi, xw = items(h)
        pi_copy(h - 1).wait_recv()
        xi += plain(piring[h - 1, 0:IS, :], piring[h - 1, IS : IS + 16, :])
        xw += plain(piring[h - 1, IS + 16 : IS + 32, :], piring[h - 1, IS + 32 :, :])
        if h < NY - 1:
            pi_start(h, xi, xw)
        else:
            out_i[...] = xi
            out_w[...] = xw[0:WS, :]

    for fn in pend.values():
        fn()
    for fn in leave:
        fn()


def finish(*refs):
    n = (len(refs) - 1) // 3
    src, dst, hold, sem = refs[:n], refs[n : 2 * n], refs[2 * n : 3 * n], refs[-1]
    inward = [pltpu.make_async_copy(src[k], hold[k], sem.at[0, k]) for k in range(n)]
    outward = [pltpu.make_async_copy(hold[k], dst[k], sem.at[1, k]) for k in range(n)]
    for cp in inward:
        cp.start()
    for k in range(n):
        inward[k].wait()
        outward[k].start()
    for cp in outward:
        cp.wait()


def local(
    W,
    NY,
    user_table,
    item_table,
    week_table,
    profile,
    feature_table,
    user_req,
    item_req,
    week_req,
    user_counts,
    item_counts,
    week_counts,
    pos_cells,
):
    UR, IR, WR = user_table.shape[0], item_table.shape[0], week_table.shape[0]
    FD = feature_table.shape[0]
    US, IS, WS = UR // (2 * NY), IR // (2 * NY), WR // (2 * NY)
    FC = FD // W
    groups = W // GROUP
    V, D = pltpu.VMEM, pltpu.SemaphoreType.DMA
    anywhere = pl.BlockSpec(memory_space=pl.ANY)
    vmem = pl.BlockSpec(memory_space=pltpu.VMEM)
    smem = pl.BlockSpec(memory_space=pltpu.SMEM)
    shapes = (
        jax.ShapeDtypeStruct((US, RANK), F32),
        jax.ShapeDtypeStruct((IS, RANK), F32),
        jax.ShapeDtypeStruct((WS, RANK), F32),
        jax.ShapeDtypeStruct((FD, RANK), F32),
    )
    outs = pl.pallas_call(
        functools.partial(kernel, W, NY),
        out_shape=shapes,
        in_specs=[anywhere] * 5 + [vmem] * 3 + [smem] * 3 + [vmem],
        out_specs=(vmem, vmem, vmem, vmem),
        scratch_shapes=[
            V((UR, RANK), BF16),
            V((IR, RANK), BF16),
            V((WR, RANK), BF16),
            V((UR, FD), BF16),
            V((FD, RANK), BF16),
            V((NY, US, FD), BF16),
            V((FD, RANK), BF16),
            V((W, 8, 128), I32),
            V((W, 8, 128), I32),
            V((W // 2 * CAPU, UR), BF16),
            V((W, MSG, RANK), BF16),
            V((W, MSG, RANK), BF16),
            V((NY, US, RANK), F32),
            V((NY - 1, US + 16, RANK), I16),
            V((NY - 1, US + 16, RANK), I16),
            V((NY - 1, IS + 48, RANK), I16),
            V((NY - 1, IS + 48, RANK), I16),
            V((RANK, FD), F32),
            V((W, FC, RANK), F32),
            V((W, FC, RANK), F32),
            V((W, FC, RANK), F32),
            V((32, 128), I32),
            V((32, 8, 128), I32),
            V((1, pos_cells.shape[1]), F32),
            V((32, 128, 128), I32),
            V((3 * BU, BI), F32),
            V((BU, BI), I32),
            V((BU, RANK), F32),
            V((32, RANK), F32),
            V((BI, RANK), BF16),
            V((RANK, BI), BF16),
            V((BU, RANK), F32),
            V((BI, RANK), F32),
            V((32, RANK), F32),
            V(((BW + PAIR) * BU, RANK), BF16),
            V((BW * BU, BI), BF16),
            V((PAIR * BU, BI), F32),
            V((PAIR * BU, BI), F32),
            V((W, CAPU + CAPX, RANK), I16),
            V((W, CAPI + CAPX, RANK), I16),
            V((W, CAPU + CAPX, RANK), I16),
            V((W, CAPI + CAPX, RANK), I16),
            V((W, CAPU + CAPX, RANK), I16),
            V((W, CAPI + CAPX, RANK), I16),
            V((1, 2 * W * CAPU), F32),
            V((1, 2 * W * CAPI), F32),
            V((1, 2 * W * CAPX), F32),
            V((1, 2 * W * CAPU), F32),
            V((1, 2 * W * CAPI), F32),
            V((1, 2 * W * CAPX), F32),
            V((2 * W * CAPU, 2 * RANK), BF16),
            V((2 * W * CAPI, 2 * RANK), BF16),
            V((2 * W * CAPX, 2 * RANK), BF16),
            D((5,)),
            D((W,)),
            D((W,)),
            D((NY + 1,)),
            D((NY + 1,)),
            D((W,)),
            D((W,)),
            D((W,)),
            D((W,)),
            D((W,)),
            D((W,)),
            D((NY - 1,)),
            D((NY - 1,)),
            D((NY - 1,)),
            D((NY - 1,)),
            D((W,)),
            D((W,)),
            D((W,)),
            D((W,)),
            D((groups,)),
            D((groups,)),
            D((groups,)),
            D((groups,)),
        ],
        compiler_params=pltpu.CompilerParams(
            collective_id=0, has_side_effects=True, vmem_limit_bytes=56 << 20
        ),
    )(
        user_table,
        item_table,
        week_table,
        profile,
        feature_table,
        user_req[0],
        item_req[0],
        jnp.swapaxes(week_req[0], 0, 1),
        user_counts,
        item_counts,
        week_counts,
        pos_cells,
    )
    return pl.pallas_call(
        finish,
        out_shape=shapes,
        in_specs=[anywhere] * len(shapes),
        out_specs=(anywhere,) * len(shapes),
        scratch_shapes=[V(a.shape, a.dtype) for a in shapes] + [D((2, len(shapes)))],
    )(*outs)

def solution(mesh):
    W, NY = mesh.shape["wide"], mesh.shape["narrow"] // 2
    both = ("wide", "narrow")
    return jax.shard_map(
        functools.partial(local, W, NY),
        mesh=mesh,
        in_specs=(
            P("wide", None),
            P("wide", None),
            P("wide", None),
            P("wide", "narrow"),
            P("narrow", None),
            P(both, None, None),
            P(both, None, None),
            P(both, None, None),
            P(both, None),
            P(both, None),
            P(both, None),
            P(both, None),
        ),
        out_specs=(P(both, None), P(both, None), P(both, None), P("narrow", None)),
        check_vma=False,
    )
```

```python
import functools

import jax
import jax.numpy as jnp
from jax import lax
from jax.experimental import pallas as pl
from jax.experimental.pallas import tpu as pltpu
from jax.sharding import PartitionSpec as P

RANK = 256
BU = 256
BI = 256
BW = 28
CAPU = 32
CAPI = 32
CAPW = 4
CAPX = 16
MSG = CAPU + CAPI + CAPX
GROUP = 4
GROUPS = (0, 1, 3, 2)
FIELDS = 12
BLOCK = 4
THIRD = 3
PAIR = 2
SIDE = 4
ORDER = (1, 4, 3, 12, 5, 15, 7, 13, 2, 8, 9, 14, 11, 6, 10)
MESH = pl.DeviceIdType.MESH
F32, BF16, I32, I16 = jnp.float32, jnp.bfloat16, jnp.int32, jnp.int16


def dot(a, b):
    return jnp.dot(a, b, preferred_element_type=F32)


def dot_nt(a, b):
    return lax.dot_general(a, b, (((1,), (1,)), ((), ())), preferred_element_type=F32)


def dot_tn(a, b):
    return lax.dot_general(a, b, (((0,), (0,)), ((), ())), preferred_element_type=F32)


def iota(shape, axis):
    return lax.broadcasted_iota(I32, shape, axis)


def flat_index(counts, owners, place, cap):
    flat, end = place, 0
    for o in range(owners):
        c = counts[0, o]
        end = end + c
        flat = flat + jnp.where(place >= end, cap - c, 0)
    return flat


def halves(q):
    high = jnp.round(q * (1.0 / 256.0))
    return high, q - 256.0 * high


def exponent(top):
    return jnp.ceil(jnp.log2(jnp.maximum(top, 2.0**-100))) - 15.0


def quantize(x, e):
    return jnp.clip(jnp.round(x * jnp.exp2(-e)), -32767.0, 32767.0)


def kernel(
    W,
    NY,
    utab,
    itab,
    wtab,
    prof,
    ftab,
    ureq,
    ireq,
    wreq,
    ucnt,
    icnt,
    wcnt,
    pos,
    out_u,
    out_i,
    out_w,
    out_f,
    uv,
    iv,
    wv,
    xv,
    fv,
    x2,
    f2,
    reqs,
    rq,
    hot,
    rowsend,
    rowbuf,
    gp,
    pusend,
    puring,
    pisend,
    piring,
    feat,
    fsend,
    frecv,
    fall,
    pos_s,
    near,
    keep,
    spread,
    cacc,
    bits,
    uf,
    wf,
    vb,
    vt,
    gu,
    gv,
    gw,
    uw,
    gg,
    mm0,
    mm1,
    umsg,
    vmsg,
    umine,
    vmine,
    utheirs,
    vtheirs,
    uid,
    iid,
    wid,
    usc,
    isc,
    wsc,
    urh,
    irh,
    wrh,
    load_sem,
    req_ss,
    req_rs,
    x_ss,
    x_rs,
    row_ss,
    row_rs,
    fr_ss,
    fr_rs,
    fa_ss,
    fa_rs,
    pu_ss,
    pu_rs,
    pi_ss,
    pi_rs,
    mu_ss,
    mu_rs,
    mv_ss,
    mv_rs,
    su_ss,
    su_rs,
    sv_ss,
    sv_rs,
):
    me = lax.axis_index("wide")
    nar = lax.axis_index("narrow")
    y, c = nar // 2, nar % 2
    step = 1 - 2 * c
    nxt = lax.rem(y + step + NY, NY) * 2 + c
    prv = lax.rem(y - step + NY, NY) * 2 + c
    sib = y * 2 + 1 - c
    UR, IR, WR = uv.shape[0], iv.shape[0], wv.shape[0]
    FD = fv.shape[0]
    US, IS, WS = UR // (2 * NY), IR // (2 * NY), WR // (2 * NY)
    FC = FD // W

    X, Z = me // SIDE, lax.rem(me, SIDE)

    def to(s):
        return lax.rem(X + s // SIDE, SIDE) * SIDE + lax.rem(Z + s % SIDE, SIDE)

    def frm(s):
        return lax.rem(X + SIDE - s // SIDE, SIDE) * SIDE + lax.rem(Z + SIDE - s % SIDE, SIDE)

    def rcopy(src, dst, ss, rs, dev):
        return pltpu.make_async_remote_copy(
            src_ref=src,
            dst_ref=dst,
            send_sem=ss,
            recv_sem=rs,
            device_id=dev,
            device_id_type=MESH,
        )

    def peers(fn):
        for s in ORDER:
            fn(s)

    leave, pend = [], {}

    loads = [
        pltpu.make_async_copy(utab, uv, load_sem.at[0]),
        pltpu.make_async_copy(itab, iv, load_sem.at[1]),
        pltpu.make_async_copy(wtab, wv, load_sem.at[2]),
        pltpu.make_async_copy(ftab, fv, load_sem.at[3]),
        pltpu.make_async_copy(prof, xv, load_sem.at[4]),
    ]
    for cp in loads:
        cp.start()
    pend["tables"] = lambda: [cp.wait() for cp in loads[:3]]
    pend["profile"] = lambda: [cp.wait() for cp in loads[3:]]
    barrier = pltpu.get_barrier_semaphore()
    peers(
        lambda s: pl.semaphore_signal(
            barrier, inc=1, device_id={"wide": to(s)}, device_id_type=MESH
        )
    )
    for n in (nxt, prv, sib):
        pl.semaphore_signal(barrier, inc=1, device_id={"narrow": n}, device_id_type=MESH)
    for kind, ids in ((0, ureq[...]), (1, ireq[...])):
        line = jnp.concatenate([ids] * (128 // ids.shape[1]), axis=1)
        for o in range(W):
            reqs[o, kind : kind + 1, :] = line[o : o + 1, :]
    used = jnp.concatenate([wreq[...], jnp.zeros((CAPX - CAPW, W), I32)], axis=0)
    used = jnp.concatenate([used] * (128 // CAPX), axis=0)
    used = jnp.swapaxes(jnp.concatenate([used] * (128 // W), axis=1), 0, 1)
    for o in range(W):
        reqs[o, 2:3, :] = used[o : o + 1, :]
        reqs[o, 3:8, :] = jnp.zeros((5, 128), I32)
    big = 1 << 30

    def least(xs):
        while len(xs) > 1:
            xs = [jnp.minimum(a, b) for a, b in zip(xs[::2], xs[1::2])]
        return xs[0]

    lines = pos.shape[1] // 128
    for k in range(lines):
        pos_s[k : k + 1, :] = pos[:, 128 * k : 128 * (k + 1)]
    near[...] = jnp.full(near.shape, big, I32)
    pt = jnp.swapaxes(
        jnp.concatenate([pos_s[...], jnp.zeros((128 - lines, 128), I32)], axis=0), 0, 1
    )
    for k in range(lines):
        spread[k] = jnp.broadcast_to(pt[:, k : k + 1], (128, 128))

    pl.semaphore_wait(barrier, W - 1 + 3)

    def req_copy(s):
        return rcopy(
            reqs.at[to(s)],
            rq.at[s],
            req_ss.at[s],
            req_rs.at[s],
            {"wide": to(s)},
        )

    peers(lambda s: req_copy(s).start())
    rq[0] = reqs[me]
    leave.append(lambda: peers(lambda s: req_copy(s).wait_send()))
    pend["rq"] = lambda: peers(lambda s: req_copy(s).wait_recv())

    def x_copy(q):
        row = pl.multiple_of((2 * q + 1 - c) * US, US)
        return rcopy(
            prof.at[pl.ds(row, US), :], x2.at[q], x_ss.at[q], x_rs.at[q], {"narrow": sib}
        )

    f_copy = rcopy(ftab, f2, x_ss.at[NY], x_rs.at[NY], {"narrow": sib})
    f_copy.start()
    for q in range(NY):
        x_copy(q).start()

    def x_wait():
        f_copy.wait_recv()
        for q in range(NY):
            x_copy(q).wait_recv()

    def x_sent():
        f_copy.wait_send()
        for q in range(NY):
            x_copy(q).wait_send()

    pend["x"] = x_wait
    leave.append(x_sent)

    def compare(k, block, masked):
        for a in range(BLOCK):
            n = block * BLOCK + a
            row = jnp.broadcast_to(pos_s[pl.ds(n, 1), :], (8, 128))
            xs = []
            for t in range(16):
                x = spread[k, 8 * t : 8 * t + 8, :] ^ row
                if masked:
                    first = k * 128 + 8 * t + iota((8, 128), 0)
                    x = jnp.where(first < n * 128 + iota((8, 128), 1), x, big)
                xs.append(x)
            near[n] = jnp.minimum(near[n], least(xs))

    def column(k, z):
        own = k // BLOCK
        stop = jnp.minimum((own // THIRD + 1) * THIRD, lines // BLOCK)
        compare(k, own, True)
        lax.fori_loop(own + 1, stop, lambda b, y: (compare(k, b, False), y)[1], 0)
        return z

    lax.fori_loop(0, lines, column, 0)
    for k in range(lines):
        keep[:, 128 * k : 128 * (k + 1)] = jnp.min(near[k].astype(F32), axis=0, keepdims=True)
    pend.pop("tables")()
    pend.pop("rq")()
    RT = jnp.swapaxes(rq[...].reshape(W * 8, 128), 0, 1)

    def row_copy(s):
        return rcopy(
            rowsend.at[s],
            rowbuf.at[me],
            row_ss.at[s],
            row_rs.at[s],
            {"wide": frm(s)},
        )

    part = W // 2
    for m in range(2):
        slots = range(m * part, (m + 1) * part)
        for table, kind, cap, first in ((uv, 0, CAPU, 0), (iv, 1, CAPI, CAPU), (wv, 2, CAPX, CAPU + CAPI)):
            rows = table.shape[0]
            for a, s in enumerate(slots):
                col = jnp.broadcast_to(RT[0:cap, 8 * s + kind : 8 * s + kind + 1], (cap, rows))
                hot[a * cap : (a + 1) * cap, 0:rows] = jnp.where(
                    col == iota((cap, rows), 1), 1.0, 0.0
                ).astype(BF16)
            got = dot(hot[0 : part * cap, 0:rows], table[...]).astype(BF16)
            rowsend[m * part : (m + 1) * part, first : first + cap, :] = got.reshape(part, cap, RANK)
        for s in ORDER:
            if s in slots:
                row_copy(s).start()
    rowbuf[me] = rowsend[0]

    def row_wait(s):
        rcopy(
            rowsend.at[s],
            rowbuf.at[to(s)],
            row_ss.at[s],
            row_rs.at[s],
            {"wide": frm(s)},
        ).wait_recv()

    leave.append(lambda: peers(lambda s: row_copy(s).wait_send()))
    pend["row"] = lambda: peers(row_wait)

    pend.pop("profile")()
    feat[...] = jnp.zeros_like(feat)

    def resid(row, x, f):
        return (dot_nt(uv[pl.ds(row, US), :], f) - x.astype(F32)).astype(BF16)

    def own_rows(q, z):
        row = pl.multiple_of((2 * q + c) * US, US)
        r = resid(row, xv[pl.ds(row, US), :], fv[...])
        feat[...] += dot_tn(uv[pl.ds(row, US), :], r)
        gp[q] = 0.0625 * dot(r, fv[...])
        row = pl.multiple_of((2 * q + 1 - c) * US, US)
        r = resid(row, xv[pl.ds(row, US), :], fv[...])
        feat[...] += dot_tn(uv[pl.ds(row, US), :], r)
        return z

    lax.fori_loop(0, NY, own_rows, 0)
    fsend[...] = (0.0625 * jnp.swapaxes(feat[...], 0, 1)).reshape(W, FC, RANK)

    def fr_copy(s):
        return rcopy(
            fsend.at[to(s)],
            frecv.at[s],
            fr_ss.at[s],
            fr_rs.at[s],
            {"wide": to(s)},
        )


    cacc[...] = jnp.zeros_like(cacc)

    def mark(n, z):
        at = pl.ds(pl.multiple_of(n * 512, 512), 512)
        p = pos[:, at]
        week, user, item = p >> 16, (p >> 8) & 255, p & 255
        part = week // FIELDS
        bit = jnp.left_shift(jnp.ones_like(week), 2 * (week - FIELDS * part))
        w = jnp.where(keep[:, at] > 0.5, bit.astype(F32), 0.0)
        row = iota((256, 512), 0)
        mine = jnp.where(row == user, 1.0, 0.0).astype(BF16)
        a = [mine * jnp.where(part == f, w, 0.0).astype(BF16) for f in range(3)]
        b = jnp.where(row == item, 1.0, 0.0).astype(BF16)
        cacc[...] += dot_nt(jnp.concatenate(a, axis=0), b)
        return z

    lax.fori_loop(0, pos.shape[1] // 512, mark, 0)

    def present(f):
        n = cacc[f * BU : (f + 1) * BU, :].astype(I32)
        return (n | (n >> 1)) & 0x555555

    bits[...] = present(0) | (present(1) << 1) | (present(2) << (2 * FIELDS))

    def pick(counts, n, cap):
        flat = flat_index(counts, W, iota((n, 1), 0), cap)
        return jnp.where(flat == iota((n, W * cap), 1), 1.0, 0.0).astype(BF16)

    pu, pv, pw = pick(ucnt, BU, CAPU), pick(icnt, BI, CAPI), pick(wcnt, 32, CAPX)

    pend.pop("row")()
    peers(lambda s: fr_copy(s).start())
    frecv[0] = fsend[me]
    leave.append(lambda: peers(lambda s: fr_copy(s).wait_send()))
    pend["fr"] = lambda: peers(lambda s: fr_copy(s).wait_recv())
    uf[...] = dot(pu, rowbuf[:, 0:CAPU, :].reshape(W * CAPU, RANK))
    vf = dot(pv, rowbuf[:, CAPU : CAPU + CAPI, :].reshape(W * CAPI, RANK))
    wf[...] = dot(pw, rowbuf[:, CAPU + CAPI : MSG, :].reshape(W * CAPX, RANK))
    vb[...] = (0.5 * vf).astype(BF16)
    vt[...] = (0.5 * jnp.swapaxes(vf, 0, 1)).astype(BF16)
    gu[...] = jnp.zeros_like(gu)
    gv[...] = jnp.zeros_like(gv)
    gw[...] = jnp.zeros_like(gw)

    def rows_of(k):
        return pl.ds(pl.multiple_of(k * BU, BU), PAIR * BU)

    def lead(k, mm):
        mixed = [(uf[...] * wf[pl.ds(k + a, 1), :]).astype(BF16) for a in range(PAIR)]
        mixed = jnp.concatenate(mixed, axis=0)
        uw[rows_of(k), :] = mixed
        mm[...] = dot(mixed, vt[...])

    def work(k, mm):
        place = jnp.where(
            k < FIELDS,
            2 * k,
            jnp.where(k < 2 * FIELDS, 2 * (k - FIELDS) + 1, 2 * (k - FIELDS)),
        )
        hits = bits[...] >> place
        parts = []
        for a in range(PAIR):
            sign = jnp.where((hits & (1 << (2 * a))) != 0, -1.0, 1.0)
            parts.append((jnp.tanh(mm[BU * a : BU * (a + 1), :]) + sign).astype(BF16))
        g = jnp.concatenate(parts, axis=0)
        gg[rows_of(k), :] = g
        q = dot(g, vb[...])
        total = gu[...]
        for a in range(PAIR):
            w, qa = wf[pl.ds(k + a, 1), :], q[BU * a : BU * (a + 1), :]
            total = total + qa * w
            gw[pl.ds(k + a, 1), :] = jnp.sum(qa * uf[...], axis=0, keepdims=True)
        gu[...] = total

    def weeks(lo, hi):
        def both(n, z):
            k = 2 * PAIR * n
            lead(k + PAIR, mm1)
            work(k, mm0)
            lead(k + 2 * PAIR, mm0)
            work(k + PAIR, mm1)
            return z

        lax.fori_loop(lo // (2 * PAIR), hi // (2 * PAIR), both, 0)

    lead(0, mm0)
    weeks(0, BW)

    def encode(g, counts, cap):
        n = g.shape[0]
        e = exponent(jnp.max(jnp.abs(g), axis=1, keepdims=True))
        high, low = halves(quantize(g, e))
        rhs = jnp.concatenate([high, low, jnp.broadcast_to(e, (n, 128))], axis=1).astype(BF16)
        flat = flat_index(counts, W, iota((1, n), 1), cap)
        sel = jnp.where(flat == iota((W * cap, n), 0), 1.0, 0.0).astype(BF16)
        got = dot(sel, rhs)
        code = (256.0 * got[:, 0:RANK] + got[:, RANK : 2 * RANK]).astype(I32)
        es = got[:, 2 * RANK :].reshape(W, cap, 128)
        es = jnp.where(iota((W, cap, 128), 1) == iota((W, cap, 128), 2) % cap, es, 0.0)
        es = jnp.sum(es, axis=1, keepdims=True).astype(I32)
        return code.reshape(W, cap, RANK), es

    def send_out(src, dst, ss, rs):
        def copy(t):
            return rcopy(src.at[to(t)], dst.at[t], ss.at[t], rs.at[t], {"wide": to(t)})

        peers(lambda t: copy(t).start())
        dst[0] = src[me]
        leave.append(lambda: peers(lambda t: copy(t).wait_send()))
        return copy

    ucode, ue = encode(gu[...], ucnt, CAPU)
    umsg[:, 0:CAPU, :] = ucode.astype(I16)
    wcode, we = encode(gw[...], wcnt, CAPX)
    shape = (W, CAPX, RANK)
    none = jnp.zeros_like(we)
    tail = wcode
    for r, left, right in (
        (8, reqs[:, 0:1, :], reqs[:, 1:2, :]),
        (9, reqs[:, 2:3, :], none),
        (10, ue, none),
        (11, we, none),
    ):
        line = jnp.broadcast_to(jnp.concatenate([left, right], axis=2), shape)
        tail = jnp.where(iota(shape, 1) == r, line, tail)
    umsg[:, CAPU:, :] = tail.astype(I16)
    mu_copy = send_out(umsg, umine, mu_ss, mu_rs)

    def value(n, z):
        at = pl.ds(pl.multiple_of(n * 4 * BU, BU), 4 * BU)
        gv[...] += dot_tn(gg[at, :], uw[at, :])
        return z

    lax.fori_loop(0, BW // 4, value, 0)
    vcode, ve = encode(0.5 * gv[...], icnt, CAPI)
    vmsg[:, 0:CAPI, :] = vcode.astype(I16)
    line = jnp.concatenate([ve, none], axis=2)
    vmsg[:, CAPI:, :] = jnp.broadcast_to(line, shape).astype(I16)
    mv_copy = send_out(vmsg, vmine, mv_ss, mv_rs)

    pend.pop("x")()

    def sib_rows(q, z):
        row = pl.multiple_of((2 * q + c) * US, US)
        gp[q] += 0.0625 * dot(resid(row, x2[q], f2[...]), f2[...])
        return z

    lax.fori_loop(0, NY, sib_rows, 0)


    pend.pop("fr")()
    total = frecv[0]
    for s in range(1, W):
        total = total + frecv[s]
    fall[me] = total

    def fa_copy(s):
        return rcopy(fall.at[me], fall.at[me], fa_ss.at[s], fa_rs.at[s], {"wide": to(s)})

    peers(lambda s: fa_copy(s).start())

    def fa_wait(s):
        rcopy(
            fall.at[me],
            fall.at[frm(s)],
            fa_ss.at[s],
            fa_rs.at[s],
            {"wide": to(s)},
        ).wait_recv()

    leave.append(lambda: peers(lambda s: fa_copy(s).wait_send()))
    pend["fa"] = lambda: peers(fa_wait)

    groups = W // GROUP

    def share_out(copy, mine, theirs, ss, rs):
        def sib_copy(g):
            at = pl.ds(g * GROUP, GROUP)
            return rcopy(mine.at[at], theirs.at[at], ss.at[g], rs.at[g], {"narrow": sib})

        for g in GROUPS:
            for t in range(g * GROUP, (g + 1) * GROUP):
                if t > 0:
                    copy(t).wait_recv()
            sib_copy(g).start()
            leave.append(lambda g=g: sib_copy(g).wait_send())
        return lambda: [sib_copy(g).wait_recv() for g in GROUPS]

    def lanes(tail_rows, r, first, cap):
        each = 128 // cap
        pieces = []
        for p in range(W // each):
            piece = jnp.zeros((1, 128), F32)
            for a in range(each):
                line = tail_rows[p * each + a, r : r + 1, first : first + 128]
                piece = jnp.where(iota((1, 128), 1) // cap == a, line, piece)
            pieces.append(piece)
        return jnp.concatenate(pieces, axis=1)

    def rows_in(buf, b, lo, cap, rhs):
        n = W * cap
        q = buf[:, lo : lo + cap, :].astype(I32).astype(F32)
        if lo > 0:
            q = jnp.where(iota(q.shape, 1) < CAPW, q, 0.0)
        high, low = halves(q.reshape(n, RANK))
        rhs[b * n : (b + 1) * n, 0:RANK] = high.astype(BF16)
        rhs[b * n : (b + 1) * n, RANK:] = low.astype(BF16)

    def unpack_u(buf, b):
        tail_rows = buf[:, CAPU:, :].astype(I32).astype(F32)
        nu, nw = slice(b * W * CAPU, (b + 1) * W * CAPU), slice(b * W * CAPX, (b + 1) * W * CAPX)
        uid[:, nu] = lanes(tail_rows, 8, 0, CAPU)
        iid[:, nu] = lanes(tail_rows, 8, 128, CAPI)
        wid[:, nw] = lanes(tail_rows, 9, 0, CAPX)
        usc[:, nu] = jnp.exp2(lanes(tail_rows, 10, 0, CAPU))
        wsc[:, nw] = jnp.exp2(lanes(tail_rows, 11, 0, CAPX))
        rows_in(buf, b, 0, CAPU, urh)
        rows_in(buf, b, CAPU, CAPX, wrh)

    def unpack_v(buf, b):
        tail_rows = buf[:, CAPI:, :].astype(I32).astype(F32)
        isc[:, b * W * CAPI : (b + 1) * W * CAPI] = jnp.exp2(lanes(tail_rows, 0, 0, CAPI))
        rows_in(buf, b, 0, CAPI, irh)

    def added(q, rows, size, ids, scale, rhs):
        row = iota((rows, ids.shape[1]), 0)
        place = row + (2 * q + c) * size
        if rows > size:
            place = jnp.where(row < size, place, -1)
        place = place.astype(F32)
        sel = jnp.where(ids[...] == place, jnp.broadcast_to(scale[...], place.shape), 0.0)
        both = dot(sel.astype(BF16), rhs[...])
        return 256.0 * both[:, 0:RANK] + both[:, RANK:]

    def pu_copy(h):
        return rcopy(pusend.at[h], puring.at[h], pu_ss.at[h], pu_rs.at[h], {"narrow": nxt})

    def pi_copy(h):
        return rcopy(pisend.at[h], piring.at[h], pi_ss.at[h], pi_rs.at[h], {"narrow": nxt})

    def coded(x):
        e = exponent(jnp.max(jnp.abs(x), axis=0, keepdims=True))
        line = jnp.broadcast_to(e, (16, RANK)).astype(I32).astype(I16)
        return quantize(x, e).astype(I32).astype(I16), line

    def plain(code, line):
        e = line.astype(I32).astype(F32)[0:1, :]
        return code.astype(I32).astype(F32) * jnp.exp2(e)

    def pu_start(h, x):
        pusend[h, 0:US, :], pusend[h, US:, :] = coded(x)
        pu_copy(h).start()
        leave.append(lambda: pu_copy(h).wait_send())

    def pi_start(h, x, w):
        pisend[h, 0:IS, :], pisend[h, IS : IS + 16, :] = coded(x)
        pisend[h, IS + 16 : IS + 32, :], pisend[h, IS + 32 :, :] = coded(w)
        pi_copy(h).start()
        leave.append(lambda: pi_copy(h).wait_send())

    def at_hop(h):
        return lax.rem(y - (h + 1) * step + 2 * NY, NY)

    def users(h):
        return added(at_hop(h), US, US, uid, usc, urh) + gp[at_hop(h)]

    def items(h):
        q = at_hop(h)
        return added(q, IS, IS, iid, isc, irh), added(q, 16, WS, wid, wsc, wrh)

    arrived = share_out(mu_copy, umine, utheirs, su_ss, su_rs)
    unpack_u(umine, 0)
    arrived()
    unpack_u(utheirs, 1)
    pu_start(0, users(0))
    arrived = share_out(mv_copy, vmine, vtheirs, sv_ss, sv_rs)
    unpack_v(vmine, 0)
    arrived()
    unpack_v(vtheirs, 1)
    pi_start(0, *items(0))
    for h in range(1, NY):
        xu = users(h)
        if h == NY - 1:
            pend.pop("fa")()
            out_f[...] = fall[...].reshape(FD, RANK)
        pu_copy(h - 1).wait_recv()
        xu += plain(puring[h - 1, 0:US, :], puring[h - 1, US:, :])
        if h < NY - 1:
            pu_start(h, xu)
        else:
            out_u[...] = xu
        xi, xw = items(h)
        pi_copy(h - 1).wait_recv()
        xi += plain(piring[h - 1, 0:IS, :], piring[h - 1, IS : IS + 16, :])
        xw += plain(piring[h - 1, IS + 16 : IS + 32, :], piring[h - 1, IS + 32 :, :])
        if h < NY - 1:
            pi_start(h, xi, xw)
        else:
            out_i[...] = xi
            out_w[...] = xw[0:WS, :]

    for fn in pend.values():
        fn()
    for fn in leave:
        fn()


def finish(*refs):
    n = (len(refs) - 1) // 3
    src, dst, hold, sem = refs[:n], refs[n : 2 * n], refs[2 * n : 3 * n], refs[-1]
    inward = [pltpu.make_async_copy(src[k], hold[k], sem.at[0, k]) for k in range(n)]
    outward = [pltpu.make_async_copy(hold[k], dst[k], sem.at[1, k]) for k in range(n)]
    for cp in inward:
        cp.start()
    for k in range(n):
        inward[k].wait()
        outward[k].start()
    for cp in outward:
        cp.wait()


def local(
    W,
    NY,
    user_table,
    item_table,
    week_table,
    profile,
    feature_table,
    user_req,
    item_req,
    week_req,
    user_counts,
    item_counts,
    week_counts,
    pos_cells,
):
    UR, IR, WR = user_table.shape[0], item_table.shape[0], week_table.shape[0]
    FD = feature_table.shape[0]
    US, IS, WS = UR // (2 * NY), IR // (2 * NY), WR // (2 * NY)
    FC = FD // W
    groups = W // GROUP
    V, D = pltpu.VMEM, pltpu.SemaphoreType.DMA
    anywhere = pl.BlockSpec(memory_space=pl.ANY)
    vmem = pl.BlockSpec(memory_space=pltpu.VMEM)
    smem = pl.BlockSpec(memory_space=pltpu.SMEM)
    shapes = (
        jax.ShapeDtypeStruct((US, RANK), F32),
        jax.ShapeDtypeStruct((IS, RANK), F32),
        jax.ShapeDtypeStruct((WS, RANK), F32),
        jax.ShapeDtypeStruct((FD, RANK), F32),
    )
    outs = pl.pallas_call(
        functools.partial(kernel, W, NY),
        out_shape=shapes,
        in_specs=[anywhere] * 5 + [vmem] * 3 + [smem] * 3 + [vmem],
        out_specs=(vmem, vmem, vmem, vmem),
        scratch_shapes=[
            V((UR, RANK), BF16),
            V((IR, RANK), BF16),
            V((WR, RANK), BF16),
            V((UR, FD), BF16),
            V((FD, RANK), BF16),
            V((NY, US, FD), BF16),
            V((FD, RANK), BF16),
            V((W, 8, 128), I32),
            V((W, 8, 128), I32),
            V((W // 2 * CAPU, UR), BF16),
            V((W, MSG, RANK), BF16),
            V((W, MSG, RANK), BF16),
            V((NY, US, RANK), F32),
            V((NY - 1, US + 16, RANK), I16),
            V((NY - 1, US + 16, RANK), I16),
            V((NY - 1, IS + 48, RANK), I16),
            V((NY - 1, IS + 48, RANK), I16),
            V((RANK, FD), F32),
            V((W, FC, RANK), F32),
            V((W, FC, RANK), F32),
            V((W, FC, RANK), F32),
            V((32, 128), I32),
            V((32, 8, 128), I32),
            V((1, pos_cells.shape[1]), F32),
            V((32, 128, 128), I32),
            V((3 * BU, BI), F32),
            V((BU, BI), I32),
            V((BU, RANK), F32),
            V((32, RANK), F32),
            V((BI, RANK), BF16),
            V((RANK, BI), BF16),
            V((BU, RANK), F32),
            V((BI, RANK), F32),
            V((32, RANK), F32),
            V(((BW + PAIR) * BU, RANK), BF16),
            V((BW * BU, BI), BF16),
            V((PAIR * BU, BI), F32),
            V((PAIR * BU, BI), F32),
            V((W, CAPU + CAPX, RANK), I16),
            V((W, CAPI + CAPX, RANK), I16),
            V((W, CAPU + CAPX, RANK), I16),
            V((W, CAPI + CAPX, RANK), I16),
            V((W, CAPU + CAPX, RANK), I16),
            V((W, CAPI + CAPX, RANK), I16),
            V((1, 2 * W * CAPU), F32),
            V((1, 2 * W * CAPI), F32),
            V((1, 2 * W * CAPX), F32),
            V((1, 2 * W * CAPU), F32),
            V((1, 2 * W * CAPI), F32),
            V((1, 2 * W * CAPX), F32),
            V((2 * W * CAPU, 2 * RANK), BF16),
            V((2 * W * CAPI, 2 * RANK), BF16),
            V((2 * W * CAPX, 2 * RANK), BF16),
            D((5,)),
            D((W,)),
            D((W,)),
            D((NY + 1,)),
            D((NY + 1,)),
            D((W,)),
            D((W,)),
            D((W,)),
            D((W,)),
            D((W,)),
            D((W,)),
            D((NY - 1,)),
            D((NY - 1,)),
            D((NY - 1,)),
            D((NY - 1,)),
            D((W,)),
            D((W,)),
            D((W,)),
            D((W,)),
            D((groups,)),
            D((groups,)),
            D((groups,)),
            D((groups,)),
        ],
        compiler_params=pltpu.CompilerParams(
            collective_id=0, has_side_effects=True, vmem_limit_bytes=56 << 20
        ),
    )(
        user_table,
        item_table,
        week_table,
        profile,
        feature_table,
        user_req[0],
        item_req[0],
        jnp.swapaxes(week_req[0], 0, 1),
        user_counts,
        item_counts,
        week_counts,
        pos_cells,
    )
    return pl.pallas_call(
        finish,
        out_shape=shapes,
        in_specs=[anywhere] * len(shapes),
        out_specs=(anywhere,) * len(shapes),
        scratch_shapes=[V(a.shape, a.dtype) for a in shapes] + [D((2, len(shapes)))],
    )(*outs)

def solution(mesh):
    W, NY = mesh.shape["wide"], mesh.shape["narrow"] // 2
    both = ("wide", "narrow")
    return jax.shard_map(
        functools.partial(local, W, NY),
        mesh=mesh,
        in_specs=(
            P("wide", None),
            P("wide", None),
            P("wide", None),
            P("wide", "narrow"),
            P("narrow", None),
            P(both, None, None),
            P(both, None, None),
            P(both, None, None),
            P(both, None),
            P(both, None),
            P(both, None),
            P(both, None),
        ),
        out_specs=(P(both, None), P(both, None), P(both, None), P("narrow", None)),
        check_vma=False,
    )
```

```python
import functools

import jax
import jax.numpy as jnp
from jax import lax
from jax.experimental import pallas as pl
from jax.experimental.pallas import tpu as pltpu
from jax.sharding import PartitionSpec as P

RANK = 256
BU = 256
BI = 256
BW = 28
CAPU = 32
CAPI = 32
CAPW = 4
CAPX = 16
MSG = CAPU + CAPI + CAPX
GROUP = 4
GROUPS = (0, 1, 3, 2)
FIELDS = 12
BLOCK = 4
THIRD = 3
PAIR = 2
SIDE = 4
ORDER = (1, 4, 3, 12, 5, 15, 7, 13, 2, 8, 9, 14, 11, 6, 10)
MESH = pl.DeviceIdType.MESH
F32, BF16, I32, I16 = jnp.float32, jnp.bfloat16, jnp.int32, jnp.int16


def dot(a, b):
    return jnp.dot(a, b, preferred_element_type=F32)


def dot_nt(a, b):
    return lax.dot_general(a, b, (((1,), (1,)), ((), ())), preferred_element_type=F32)


def dot_tn(a, b):
    return lax.dot_general(a, b, (((0,), (0,)), ((), ())), preferred_element_type=F32)


def iota(shape, axis):
    return lax.broadcasted_iota(I32, shape, axis)


def flat_index(counts, owners, place, cap):
    flat, end = place, 0
    for o in range(owners):
        c = counts[0, o]
        end = end + c
        flat = flat + jnp.where(place >= end, cap - c, 0)
    return flat


def halves(q):
    high = jnp.round(q * (1.0 / 256.0))
    return high, q - 256.0 * high


def exponent(top):
    return jnp.ceil(jnp.log2(jnp.maximum(top, 2.0**-100))) - 15.0


def quantize(x, e):
    return jnp.clip(jnp.round(x * jnp.exp2(-e)), -32767.0, 32767.0)


def kernel(
    W,
    NY,
    utab,
    itab,
    wtab,
    prof,
    ftab,
    ureq,
    ireq,
    wreq,
    ucnt,
    icnt,
    wcnt,
    pos,
    out_u,
    out_i,
    out_w,
    out_f,
    uv,
    iv,
    wv,
    xv,
    fv,
    x2,
    f2,
    reqs,
    rq,
    hot,
    rowsend,
    rowbuf,
    gp,
    pusend,
    puring,
    pisend,
    piring,
    feat,
    fsend,
    frecv,
    fall,
    pos_s,
    near,
    keep,
    spread,
    cacc,
    bits,
    uf,
    wf,
    vb,
    vt,
    gu,
    gv,
    gw,
    uw,
    gg,
    mm0,
    mm1,
    umsg,
    vmsg,
    umine,
    vmine,
    utheirs,
    vtheirs,
    uid,
    iid,
    wid,
    usc,
    isc,
    wsc,
    urh,
    irh,
    wrh,
    load_sem,
    req_ss,
    req_rs,
    x_ss,
    x_rs,
    row_ss,
    row_rs,
    fr_ss,
    fr_rs,
    fa_ss,
    fa_rs,
    pu_ss,
    pu_rs,
    pi_ss,
    pi_rs,
    mu_ss,
    mu_rs,
    mv_ss,
    mv_rs,
    su_ss,
    su_rs,
    sv_ss,
    sv_rs,
):
    me = lax.axis_index("wide")
    nar = lax.axis_index("narrow")
    y, c = nar // 2, nar % 2
    step = 1 - 2 * c
    nxt = lax.rem(y + step + NY, NY) * 2 + c
    prv = lax.rem(y - step + NY, NY) * 2 + c
    sib = y * 2 + 1 - c
    UR, IR, WR = uv.shape[0], iv.shape[0], wv.shape[0]
    FD = fv.shape[0]
    US, IS, WS = UR // (2 * NY), IR // (2 * NY), WR // (2 * NY)
    FC = FD // W

    X, Z = me // SIDE, lax.rem(me, SIDE)

    def to(s):
        return lax.rem(X + s // SIDE, SIDE) * SIDE + lax.rem(Z + s % SIDE, SIDE)

    def frm(s):
        return lax.rem(X + SIDE - s // SIDE, SIDE) * SIDE + lax.rem(Z + SIDE - s % SIDE, SIDE)

    def rcopy(src, dst, ss, rs, dev):
        return pltpu.make_async_remote_copy(
            src_ref=src,
            dst_ref=dst,
            send_sem=ss,
            recv_sem=rs,
            device_id=dev,
            device_id_type=MESH,
        )

    def peers(fn):
        for s in ORDER:
            fn(s)

    leave, pend = [], {}

    loads = [
        pltpu.make_async_copy(utab, uv, load_sem.at[0]),
        pltpu.make_async_copy(itab, iv, load_sem.at[1]),
        pltpu.make_async_copy(wtab, wv, load_sem.at[2]),
        pltpu.make_async_copy(ftab, fv, load_sem.at[3]),
        pltpu.make_async_copy(prof, xv, load_sem.at[4]),
    ]
    for cp in loads:
        cp.start()
    pend["tables"] = lambda: [cp.wait() for cp in loads[:3]]
    pend["profile"] = lambda: [cp.wait() for cp in loads[3:]]
    barrier = pltpu.get_barrier_semaphore()
    peers(
        lambda s: pl.semaphore_signal(
            barrier, inc=1, device_id={"wide": to(s)}, device_id_type=MESH
        )
    )
    for n in (nxt, prv, sib):
        pl.semaphore_signal(barrier, inc=1, device_id={"narrow": n}, device_id_type=MESH)
    for kind, ids in ((0, ureq[...]), (1, ireq[...])):
        line = jnp.concatenate([ids] * (128 // ids.shape[1]), axis=1)
        for o in range(W):
            reqs[o, kind : kind + 1, :] = line[o : o + 1, :]
    used = jnp.concatenate([wreq[...], jnp.zeros((CAPX - CAPW, W), I32)], axis=0)
    used = jnp.concatenate([used] * (128 // CAPX), axis=0)
    used = jnp.swapaxes(jnp.concatenate([used] * (128 // W), axis=1), 0, 1)
    for o in range(W):
        reqs[o, 2:3, :] = used[o : o + 1, :]
        reqs[o, 3:8, :] = jnp.zeros((5, 128), I32)
    big = 1 << 30

    def least(xs):
        while len(xs) > 1:
            xs = [jnp.minimum(a, b) for a, b in zip(xs[::2], xs[1::2])]
        return xs[0]

    lines = pos.shape[1] // 128
    for k in range(lines):
        pos_s[k : k + 1, :] = pos[:, 128 * k : 128 * (k + 1)]
    near[...] = jnp.full(near.shape, big, I32)
    pt = jnp.swapaxes(
        jnp.concatenate([pos_s[...], jnp.zeros((128 - lines, 128), I32)], axis=0), 0, 1
    )
    for k in range(lines):
        spread[k] = jnp.broadcast_to(pt[:, k : k + 1], (128, 128))

    pl.semaphore_wait(barrier, W - 1 + 3)

    def req_copy(s):
        return rcopy(
            reqs.at[to(s)],
            rq.at[s],
            req_ss.at[s],
            req_rs.at[s],
            {"wide": to(s)},
        )

    peers(lambda s: req_copy(s).start())
    rq[0] = reqs[me]
    leave.append(lambda: peers(lambda s: req_copy(s).wait_send()))
    pend["rq"] = lambda: peers(lambda s: req_copy(s).wait_recv())

    def x_copy(q):
        row = pl.multiple_of((2 * q + 1 - c) * US, US)
        return rcopy(
            prof.at[pl.ds(row, US), :], x2.at[q], x_ss.at[q], x_rs.at[q], {"narrow": sib}
        )

    f_copy = rcopy(ftab, f2, x_ss.at[NY], x_rs.at[NY], {"narrow": sib})
    f_copy.start()
    for q in range(NY):
        x_copy(q).start()

    def x_wait():
        f_copy.wait_recv()
        for q in range(NY):
            x_copy(q).wait_recv()

    def x_sent():
        f_copy.wait_send()
        for q in range(NY):
            x_copy(q).wait_send()

    pend["x"] = x_wait
    leave.append(x_sent)

    def compare(k, block, masked):
        for a in range(BLOCK):
            n = block * BLOCK + a
            row = jnp.broadcast_to(pos_s[pl.ds(n, 1), :], (8, 128))
            xs = []
            for t in range(16):
                x = spread[k, 8 * t : 8 * t + 8, :] ^ row
                if masked:
                    first = k * 128 + 8 * t + iota((8, 128), 0)
                    x = jnp.where(first < n * 128 + iota((8, 128), 1), x, big)
                xs.append(x)
            near[n] = jnp.minimum(near[n], least(xs))

    def column(k, z):
        own = k // BLOCK
        stop = jnp.minimum((own // THIRD + 1) * THIRD, lines // BLOCK)
        compare(k, own, True)
        lax.fori_loop(own + 1, stop, lambda b, y: (compare(k, b, False), y)[1], 0)
        return z

    lax.fori_loop(0, lines, column, 0)
    for k in range(lines):
        keep[:, 128 * k : 128 * (k + 1)] = jnp.min(near[k].astype(F32), axis=0, keepdims=True)
    pend.pop("tables")()
    pend.pop("rq")()
    RT = jnp.swapaxes(rq[...].reshape(W * 8, 128), 0, 1)

    def row_copy(s):
        return rcopy(
            rowsend.at[s],
            rowbuf.at[me],
            row_ss.at[s],
            row_rs.at[s],
            {"wide": frm(s)},
        )

    part = W // 2
    for m in range(2):
        slots = range(m * part, (m + 1) * part)
        for table, kind, cap, first in ((uv, 0, CAPU, 0), (iv, 1, CAPI, CAPU), (wv, 2, CAPX, CAPU + CAPI)):
            rows = table.shape[0]
            for a, s in enumerate(slots):
                col = jnp.broadcast_to(RT[0:cap, 8 * s + kind : 8 * s + kind + 1], (cap, rows))
                hot[a * cap : (a + 1) * cap, 0:rows] = jnp.where(
                    col == iota((cap, rows), 1), 1.0, 0.0
                ).astype(BF16)
            got = dot(hot[0 : part * cap, 0:rows], table[...]).astype(BF16)
            rowsend[m * part : (m + 1) * part, first : first + cap, :] = got.reshape(part, cap, RANK)
        for s in ORDER:
            if s in slots:
                row_copy(s).start()
    rowbuf[me] = rowsend[0]

    def row_wait(s):
        rcopy(
            rowsend.at[s],
            rowbuf.at[to(s)],
            row_ss.at[s],
            row_rs.at[s],
            {"wide": frm(s)},
        ).wait_recv()

    leave.append(lambda: peers(lambda s: row_copy(s).wait_send()))
    pend["row"] = lambda: peers(row_wait)

    pend.pop("profile")()
    feat[...] = jnp.zeros_like(feat)

    def resid(row, x, f):
        return (dot_nt(uv[pl.ds(row, US), :], f) - x.astype(F32)).astype(BF16)

    def own_rows(q, z):
        row = pl.multiple_of((2 * q + c) * US, US)
        r = resid(row, xv[pl.ds(row, US), :], fv[...])
        feat[...] += dot_tn(uv[pl.ds(row, US), :], r)
        gp[q] = 0.0625 * dot(r, fv[...])
        row = pl.multiple_of((2 * q + 1 - c) * US, US)
        r = resid(row, xv[pl.ds(row, US), :], fv[...])
        feat[...] += dot_tn(uv[pl.ds(row, US), :], r)
        return z

    lax.fori_loop(0, NY, own_rows, 0)
    fsend[...] = (0.0625 * jnp.swapaxes(feat[...], 0, 1)).reshape(W, FC, RANK)

    def fr_copy(s):
        return rcopy(
            fsend.at[to(s)],
            frecv.at[s],
            fr_ss.at[s],
            fr_rs.at[s],
            {"wide": to(s)},
        )


    cacc[...] = jnp.zeros_like(cacc)

    def mark(n, z):
        at = pl.ds(pl.multiple_of(n * 512, 512), 512)
        p = pos[:, at]
        week, user, item = p >> 16, (p >> 8) & 255, p & 255
        part = week // FIELDS
        bit = jnp.left_shift(jnp.ones_like(week), 2 * (week - FIELDS * part))
        w = jnp.where(keep[:, at] > 0.5, bit.astype(F32), 0.0)
        row = iota((256, 512), 0)
        mine = jnp.where(row == user, 1.0, 0.0).astype(BF16)
        a = [mine * jnp.where(part == f, w, 0.0).astype(BF16) for f in range(3)]
        b = jnp.where(row == item, 1.0, 0.0).astype(BF16)
        cacc[...] += dot_nt(jnp.concatenate(a, axis=0), b)
        return z

    lax.fori_loop(0, pos.shape[1] // 512, mark, 0)

    def present(f):
        n = cacc[f * BU : (f + 1) * BU, :].astype(I32)
        return (n | (n >> 1)) & 0x555555

    bits[...] = present(0) | (present(1) << 1) | (present(2) << (2 * FIELDS))

    def pick(counts, n, cap):
        flat = flat_index(counts, W, iota((n, 1), 0), cap)
        return jnp.where(flat == iota((n, W * cap), 1), 1.0, 0.0).astype(BF16)

    pu, pv, pw = pick(ucnt, BU, CAPU), pick(icnt, BI, CAPI), pick(wcnt, 32, CAPX)

    pend.pop("row")()
    peers(lambda s: fr_copy(s).start())
    frecv[0] = fsend[me]
    leave.append(lambda: peers(lambda s: fr_copy(s).wait_send()))
    pend["fr"] = lambda: peers(lambda s: fr_copy(s).wait_recv())
    uf[...] = dot(pu, rowbuf[:, 0:CAPU, :].reshape(W * CAPU, RANK))
    vf = dot(pv, rowbuf[:, CAPU : CAPU + CAPI, :].reshape(W * CAPI, RANK))
    wf[...] = dot(pw, rowbuf[:, CAPU + CAPI : MSG, :].reshape(W * CAPX, RANK))
    vb[...] = (0.5 * vf).astype(BF16)
    vt[...] = (0.5 * jnp.swapaxes(vf, 0, 1)).astype(BF16)
    gu[...] = jnp.zeros_like(gu)
    gv[...] = jnp.zeros_like(gv)
    gw[...] = jnp.zeros_like(gw)

    def rows_of(k):
        return pl.ds(pl.multiple_of(k * BU, BU), PAIR * BU)

    def lead(k, mm):
        mixed = [(uf[...] * wf[pl.ds(k + a, 1), :]).astype(BF16) for a in range(PAIR)]
        mixed = jnp.concatenate(mixed, axis=0)
        uw[rows_of(k), :] = mixed
        mm[...] = dot(mixed, vt[...])

    def work(k, mm):
        place = jnp.where(
            k < FIELDS,
            2 * k,
            jnp.where(k < 2 * FIELDS, 2 * (k - FIELDS) + 1, 2 * (k - FIELDS)),
        )
        hits = bits[...] >> place
        parts = []
        for a in range(PAIR):
            sign = jnp.where((hits & (1 << (2 * a))) != 0, -1.0, 1.0)
            parts.append((jnp.tanh(mm[BU * a : BU * (a + 1), :]) + sign).astype(BF16))
        g = jnp.concatenate(parts, axis=0)
        gg[rows_of(k), :] = g
        q = dot(g, vb[...])
        total = gu[...]
        for a in range(PAIR):
            w, qa = wf[pl.ds(k + a, 1), :], q[BU * a : BU * (a + 1), :]
            total = total + qa * w
            gw[pl.ds(k + a, 1), :] = jnp.sum(qa * uf[...], axis=0, keepdims=True)
        gu[...] = total

    def weeks(lo, hi):
        def both(n, z):
            k = 2 * PAIR * n
            lead(k + PAIR, mm1)
            work(k, mm0)
            lead(k + 2 * PAIR, mm0)
            work(k + PAIR, mm1)
            return z

        lax.fori_loop(lo // (2 * PAIR), hi // (2 * PAIR), both, 0)

    lead(0, mm0)
    weeks(0, BW)

    def encode(g, counts, cap):
        n = g.shape[0]
        e = exponent(jnp.max(jnp.abs(g), axis=1, keepdims=True))
        high, low = halves(quantize(g, e))
        rhs = jnp.concatenate([high, low, jnp.broadcast_to(e, (n, 128))], axis=1).astype(BF16)
        flat = flat_index(counts, W, iota((1, n), 1), cap)
        sel = jnp.where(flat == iota((W * cap, n), 0), 1.0, 0.0).astype(BF16)
        got = dot(sel, rhs)
        code = (256.0 * got[:, 0:RANK] + got[:, RANK : 2 * RANK]).astype(I32)
        es = got[:, 2 * RANK :].reshape(W, cap, 128)
        es = jnp.where(iota((W, cap, 128), 1) == iota((W, cap, 128), 2) % cap, es, 0.0)
        es = jnp.sum(es, axis=1, keepdims=True).astype(I32)
        return code.reshape(W, cap, RANK), es

    def send_out(src, dst, ss, rs):
        def copy(t):
            return rcopy(src.at[to(t)], dst.at[t], ss.at[t], rs.at[t], {"wide": to(t)})

        peers(lambda t: copy(t).start())
        dst[0] = src[me]
        leave.append(lambda: peers(lambda t: copy(t).wait_send()))
        return copy

    ucode, ue = encode(gu[...], ucnt, CAPU)
    umsg[:, 0:CAPU, :] = ucode.astype(I16)
    wcode, we = encode(gw[...], wcnt, CAPX)
    shape = (W, CAPX, RANK)
    none = jnp.zeros_like(we)
    tail = wcode
    for r, left, right in (
        (8, reqs[:, 0:1, :], reqs[:, 1:2, :]),
        (9, reqs[:, 2:3, :], none),
        (10, ue, none),
        (11, we, none),
    ):
        line = jnp.broadcast_to(jnp.concatenate([left, right], axis=2), shape)
        tail = jnp.where(iota(shape, 1) == r, line, tail)
    umsg[:, CAPU:, :] = tail.astype(I16)
    mu_copy = send_out(umsg, umine, mu_ss, mu_rs)

    def value(n, z):
        at = pl.ds(pl.multiple_of(n * 4 * BU, BU), 4 * BU)
        gv[...] += dot_tn(gg[at, :], uw[at, :])
        return z

    lax.fori_loop(0, BW // 4, value, 0)
    vcode, ve = encode(0.5 * gv[...], icnt, CAPI)
    vmsg[:, 0:CAPI, :] = vcode.astype(I16)
    line = jnp.concatenate([ve, none], axis=2)
    vmsg[:, CAPI:, :] = jnp.broadcast_to(line, shape).astype(I16)
    mv_copy = send_out(vmsg, vmine, mv_ss, mv_rs)

    pend.pop("x")()

    def sib_rows(q, z):
        row = pl.multiple_of((2 * q + c) * US, US)
        gp[q] += 0.0625 * dot(resid(row, x2[q], f2[...]), f2[...])
        return z

    lax.fori_loop(0, NY, sib_rows, 0)


    groups = W // GROUP

    def share_out(copy, mine, theirs, ss, rs):
        def sib_copy(g):
            at = pl.ds(g * GROUP, GROUP)
            return rcopy(mine.at[at], theirs.at[at], ss.at[g], rs.at[g], {"narrow": sib})

        for g in GROUPS:
            for t in range(g * GROUP, (g + 1) * GROUP):
                if t > 0:
                    copy(t).wait_recv()
            sib_copy(g).start()
            leave.append(lambda g=g: sib_copy(g).wait_send())
        return lambda: [sib_copy(g).wait_recv() for g in GROUPS]

    def lanes(tail_rows, r, first, cap):
        each = 128 // cap
        pieces = []
        for p in range(W // each):
            piece = jnp.zeros((1, 128), F32)
            for a in range(each):
                line = tail_rows[p * each + a, r : r + 1, first : first + 128]
                piece = jnp.where(iota((1, 128), 1) // cap == a, line, piece)
            pieces.append(piece)
        return jnp.concatenate(pieces, axis=1)

    def rows_in(buf, b, lo, cap, rhs):
        n = W * cap
        q = buf[:, lo : lo + cap, :].astype(I32).astype(F32)
        if lo > 0:
            q = jnp.where(iota(q.shape, 1) < CAPW, q, 0.0)
        high, low = halves(q.reshape(n, RANK))
        rhs[b * n : (b + 1) * n, 0:RANK] = high.astype(BF16)
        rhs[b * n : (b + 1) * n, RANK:] = low.astype(BF16)

    def unpack_u(buf, b):
        tail_rows = buf[:, CAPU:, :].astype(I32).astype(F32)
        nu, nw = slice(b * W * CAPU, (b + 1) * W * CAPU), slice(b * W * CAPX, (b + 1) * W * CAPX)
        uid[:, nu] = lanes(tail_rows, 8, 0, CAPU)
        iid[:, nu] = lanes(tail_rows, 8, 128, CAPI)
        wid[:, nw] = lanes(tail_rows, 9, 0, CAPX)
        usc[:, nu] = jnp.exp2(lanes(tail_rows, 10, 0, CAPU))
        wsc[:, nw] = jnp.exp2(lanes(tail_rows, 11, 0, CAPX))
        rows_in(buf, b, 0, CAPU, urh)
        rows_in(buf, b, CAPU, CAPX, wrh)

    def unpack_v(buf, b):
        tail_rows = buf[:, CAPI:, :].astype(I32).astype(F32)
        isc[:, b * W * CAPI : (b + 1) * W * CAPI] = jnp.exp2(lanes(tail_rows, 0, 0, CAPI))
        rows_in(buf, b, 0, CAPI, irh)

    def added(q, rows, size, ids, scale, rhs):
        row = iota((rows, ids.shape[1]), 0)
        place = row + (2 * q + c) * size
        if rows > size:
            place = jnp.where(row < size, place, -1)
        place = place.astype(F32)
        sel = jnp.where(ids[...] == place, jnp.broadcast_to(scale[...], place.shape), 0.0)
        both = dot(sel.astype(BF16), rhs[...])
        return 256.0 * both[:, 0:RANK] + both[:, RANK:]

    def pu_copy(h):
        return rcopy(pusend.at[h], puring.at[h], pu_ss.at[h], pu_rs.at[h], {"narrow": nxt})

    def pi_copy(h):
        return rcopy(pisend.at[h], piring.at[h], pi_ss.at[h], pi_rs.at[h], {"narrow": nxt})

    def coded(x):
        e = exponent(jnp.max(jnp.abs(x), axis=0, keepdims=True))
        line = jnp.broadcast_to(e, (16, RANK)).astype(I32).astype(I16)
        return quantize(x, e).astype(I32).astype(I16), line

    def plain(code, line):
        e = line.astype(I32).astype(F32)[0:1, :]
        return code.astype(I32).astype(F32) * jnp.exp2(e)

    def pu_start(h, x):
        pusend[h, 0:US, :], pusend[h, US:, :] = coded(x)
        pu_copy(h).start()
        leave.append(lambda: pu_copy(h).wait_send())

    def pi_start(h, x, w):
        pisend[h, 0:IS, :], pisend[h, IS : IS + 16, :] = coded(x)
        pisend[h, IS + 16 : IS + 32, :], pisend[h, IS + 32 :, :] = coded(w)
        pi_copy(h).start()
        leave.append(lambda: pi_copy(h).wait_send())

    def at_hop(h):
        return lax.rem(y - (h + 1) * step + 2 * NY, NY)

    def users(h):
        return added(at_hop(h), US, US, uid, usc, urh) + gp[at_hop(h)]

    def items(h):
        q = at_hop(h)
        return added(q, IS, IS, iid, isc, irh), added(q, 16, WS, wid, wsc, wrh)

    arrived = share_out(mu_copy, umine, utheirs, su_ss, su_rs)
    unpack_u(umine, 0)
    arrived()
    unpack_u(utheirs, 1)
    pu_start(0, users(0))

    pend.pop("fr")()
    total = frecv[0]
    for s in range(1, W):
        total = total + frecv[s]
    fall[me] = total

    def fa_copy(s):
        return rcopy(fall.at[me], fall.at[me], fa_ss.at[s], fa_rs.at[s], {"wide": to(s)})

    peers(lambda s: fa_copy(s).start())

    def fa_wait(s):
        rcopy(
            fall.at[me],
            fall.at[frm(s)],
            fa_ss.at[s],
            fa_rs.at[s],
            {"wide": to(s)},
        ).wait_recv()

    leave.append(lambda: peers(lambda s: fa_copy(s).wait_send()))
    pend["fa"] = lambda: peers(fa_wait)
    arrived = share_out(mv_copy, vmine, vtheirs, sv_ss, sv_rs)
    unpack_v(vmine, 0)
    arrived()
    unpack_v(vtheirs, 1)
    pi_start(0, *items(0))
    for h in range(1, NY):
        xu = users(h)
        if h == NY - 1:
            pend.pop("fa")()
            out_f[...] = fall[...].reshape(FD, RANK)
        pu_copy(h - 1).wait_recv()
        xu += plain(puring[h - 1, 0:US, :], puring[h - 1, US:, :])
        if h < NY - 1:
            pu_start(h, xu)
        else:
            out_u[...] = xu
        xi, xw = items(h)
        pi_copy(h - 1).wait_recv()
        xi += plain(piring[h - 1, 0:IS, :], piring[h - 1, IS : IS + 16, :])
        xw += plain(piring[h - 1, IS + 16 : IS + 32, :], piring[h - 1, IS + 32 :, :])
        if h < NY - 1:
            pi_start(h, xi, xw)
        else:
            out_i[...] = xi
            out_w[...] = xw[0:WS, :]

    for fn in pend.values():
        fn()
    for fn in leave:
        fn()


def finish(*refs):
    n = (len(refs) - 1) // 3
    src, dst, hold, sem = refs[:n], refs[n : 2 * n], refs[2 * n : 3 * n], refs[-1]
    inward = [pltpu.make_async_copy(src[k], hold[k], sem.at[0, k]) for k in range(n)]
    outward = [pltpu.make_async_copy(hold[k], dst[k], sem.at[1, k]) for k in range(n)]
    for cp in inward:
        cp.start()
    for k in range(n):
        inward[k].wait()
        outward[k].start()
    for cp in outward:
        cp.wait()


def local(
    W,
    NY,
    user_table,
    item_table,
    week_table,
    profile,
    feature_table,
    user_req,
    item_req,
    week_req,
    user_counts,
    item_counts,
    week_counts,
    pos_cells,
):
    UR, IR, WR = user_table.shape[0], item_table.shape[0], week_table.shape[0]
    FD = feature_table.shape[0]
    US, IS, WS = UR // (2 * NY), IR // (2 * NY), WR // (2 * NY)
    FC = FD // W
    groups = W // GROUP
    V, D = pltpu.VMEM, pltpu.SemaphoreType.DMA
    anywhere = pl.BlockSpec(memory_space=pl.ANY)
    vmem = pl.BlockSpec(memory_space=pltpu.VMEM)
    smem = pl.BlockSpec(memory_space=pltpu.SMEM)
    shapes = (
        jax.ShapeDtypeStruct((US, RANK), F32),
        jax.ShapeDtypeStruct((IS, RANK), F32),
        jax.ShapeDtypeStruct((WS, RANK), F32),
        jax.ShapeDtypeStruct((FD, RANK), F32),
    )
    outs = pl.pallas_call(
        functools.partial(kernel, W, NY),
        out_shape=shapes,
        in_specs=[anywhere] * 5 + [vmem] * 3 + [smem] * 3 + [vmem],
        out_specs=(vmem, vmem, vmem, vmem),
        scratch_shapes=[
            V((UR, RANK), BF16),
            V((IR, RANK), BF16),
            V((WR, RANK), BF16),
            V((UR, FD), BF16),
            V((FD, RANK), BF16),
            V((NY, US, FD), BF16),
            V((FD, RANK), BF16),
            V((W, 8, 128), I32),
            V((W, 8, 128), I32),
            V((W // 2 * CAPU, UR), BF16),
            V((W, MSG, RANK), BF16),
            V((W, MSG, RANK), BF16),
            V((NY, US, RANK), F32),
            V((NY - 1, US + 16, RANK), I16),
            V((NY - 1, US + 16, RANK), I16),
            V((NY - 1, IS + 48, RANK), I16),
            V((NY - 1, IS + 48, RANK), I16),
            V((RANK, FD), F32),
            V((W, FC, RANK), F32),
            V((W, FC, RANK), F32),
            V((W, FC, RANK), F32),
            V((32, 128), I32),
            V((32, 8, 128), I32),
            V((1, pos_cells.shape[1]), F32),
            V((32, 128, 128), I32),
            V((3 * BU, BI), F32),
            V((BU, BI), I32),
            V((BU, RANK), F32),
            V((32, RANK), F32),
            V((BI, RANK), BF16),
            V((RANK, BI), BF16),
            V((BU, RANK), F32),
            V((BI, RANK), F32),
            V((32, RANK), F32),
            V(((BW + PAIR) * BU, RANK), BF16),
            V((BW * BU, BI), BF16),
            V((PAIR * BU, BI), F32),
            V((PAIR * BU, BI), F32),
            V((W, CAPU + CAPX, RANK), I16),
            V((W, CAPI + CAPX, RANK), I16),
            V((W, CAPU + CAPX, RANK), I16),
            V((W, CAPI + CAPX, RANK), I16),
            V((W, CAPU + CAPX, RANK), I16),
            V((W, CAPI + CAPX, RANK), I16),
            V((1, 2 * W * CAPU), F32),
            V((1, 2 * W * CAPI), F32),
            V((1, 2 * W * CAPX), F32),
            V((1, 2 * W * CAPU), F32),
            V((1, 2 * W * CAPI), F32),
            V((1, 2 * W * CAPX), F32),
            V((2 * W * CAPU, 2 * RANK), BF16),
            V((2 * W * CAPI, 2 * RANK), BF16),
            V((2 * W * CAPX, 2 * RANK), BF16),
            D((5,)),
            D((W,)),
            D((W,)),
            D((NY + 1,)),
            D((NY + 1,)),
            D((W,)),
            D((W,)),
            D((W,)),
            D((W,)),
            D((W,)),
            D((W,)),
            D((NY - 1,)),
            D((NY - 1,)),
            D((NY - 1,)),
            D((NY - 1,)),
            D((W,)),
            D((W,)),
            D((W,)),
            D((W,)),
            D((groups,)),
            D((groups,)),
            D((groups,)),
            D((groups,)),
        ],
        compiler_params=pltpu.CompilerParams(
            collective_id=0, has_side_effects=True, vmem_limit_bytes=56 << 20
        ),
    )(
        user_table,
        item_table,
        week_table,
        profile,
        feature_table,
        user_req[0],
        item_req[0],
        jnp.swapaxes(week_req[0], 0, 1),
        user_counts,
        item_counts,
        week_counts,
        pos_cells,
    )
    return pl.pallas_call(
        finish,
        out_shape=shapes,
        in_specs=[anywhere] * len(shapes),
        out_specs=(anywhere,) * len(shapes),
        scratch_shapes=[V(a.shape, a.dtype) for a in shapes] + [D((2, len(shapes)))],
    )(*outs)

def solution(mesh):
    W, NY = mesh.shape["wide"], mesh.shape["narrow"] // 2
    both = ("wide", "narrow")
    return jax.shard_map(
        functools.partial(local, W, NY),
        mesh=mesh,
        in_specs=(
            P("wide", None),
            P("wide", None),
            P("wide", None),
            P("wide", "narrow"),
            P("narrow", None),
            P(both, None, None),
            P(both, None, None),
            P(both, None, None),
            P(both, None),
            P(both, None),
            P(both, None),
            P(both, None),
        ),
        out_specs=(P(both, None), P(both, None), P(both, None), P("narrow", None)),
        check_vma=False,
    )
```
